256 devices in a mesh: row: 16 (over x, y), col: 16 (over z, core).
Axes of the slice: x: 4, y: 4, z: 8, core: 2. Of those that a mesh axis runs over, the one named last changes fastest.
Arguments:
- start_block: float32 [65536, 128], P(('row', 'col')), may hold values from -6 to 6
- vertex_scale: float32 [65536], P(('row', 'col')), may hold values from 0.015625 to 0.0625
- adj_tiles: bfloat16 [16, 16, 64, 128, 128], P('row', 'col'), may hold values from 0 to 1
- tile_row: int32 [16, 16, 64], P('row', 'col'), may hold values from 0 to 31
- tile_col: int32 [16, 16, 64], P('row', 'col'), may hold values from 0 to 31
- live_count: int32 [16, 16], P('row', 'col'), may hold values from 16 to 64, as said below
- rotation_first: float32 [256, 128], replicated, may hold values from -0.375 to 0.375
- rotation_second: float32 [384, 128], replicated, may hold values from -0.3125 to 0.3125
Outputs:
- final_block: float32 [65536, 128], P(('row', 'col'))
- final_image: float32 [65536, 128], P(('row', 'col'))
The draws below stay inside these ranges and needn't reach their ends.
Inputs may be any that keep to these rules, and one draw needn't show every extreme that they name: Slots from live_count on are ignored; at least one device has all 64 slots live in every draw.
All inputs are finite; a program needn't handle non-finite values.
Results may differ from the reference program's by a relative error of at most 0.01.
Values may be sent and summed in bfloat16 or wider, within the bound.
A program may use at most 64 MiB of HBM per device.

```python
import math
import jax
import jax.numpy as jnp
from jax import lax

K = 128
TB = 128
SUB = 256
TILES = 64
VERTS = 65536
N_ROW = 16
N_COL = 16


def draw_live_count(key, part):
    first_key, second_key = jax.random.split(jax.random.fold_in(key, 11))
    devices_all = N_ROW * N_COL
    reduced = TILES - jax.random.randint(first_key, (devices_all,), 0, 3 * TILES // 4 + 1)
    fullest = jax.random.randint(second_key, (), 0, devices_all)
    counts = jnp.where(jnp.arange(devices_all) == fullest, TILES, reduced)
    return counts.reshape(N_ROW, N_COL).astype(jnp.int32)


def place_ends(array, stream_key, smallest, high):
    index_at = [jax.random.randint(jax.random.fold_in(stream_key, axis), (), 0, length) for axis, length in enumerate(array.shape)]
    widest = array.shape.index(max(array.shape))
    beside = index_at[:widest] + [(index_at[widest] + 1) % array.shape[widest]] + index_at[widest + 1:]
    return array.at[tuple(index_at)].set(smallest).at[tuple(beside)].set(high)


def level_of(key, extent, cuts, low, largest):
    def one(axis_at, shards_of):
        heights = jax.random.uniform(jax.random.fold_in(jax.random.fold_in(key, 6), axis_at), (shards_of,), jnp.float32, low / len(cuts), largest / len(cuts))
        return jnp.repeat(jnp.exp(heights), extent[axis_at] // shards_of).reshape((-1,) + (1,) * (len(extent) - axis_at - 1))

    gain = one(*cuts[0])
    for cut in cuts[1:]:
        gain = gain * one(*cut)
    return gain


def bell_draw(own_key, dims, scale, reach, shards=(), held_as=jnp.bfloat16):
    values = jax.random.normal(own_key, dims, jnp.float32) * scale
    if len(shards) > 0:
        values = level_of(own_key, dims, shards, -0.22, 0.18) * values
    return jnp.clip(values, min=-reach, max=reach).astype(held_as)


def setup_inputs(seed: int = 0) -> dict:
    seeds = jax.random.split(jax.random.key(seed), 9)
    return {
        "start_block": bell_draw(seeds[0], (VERTS, K), 1.0, 6.0, ((0, 256),), jnp.float32),
        "vertex_scale": jnp.clip(jnp.exp(math.log(0.0625) - 1.3862944 * jax.random.uniform(seeds[1], (VERTS,), jnp.float32) ** level_of(seeds[1], (VERTS,), ((0, 256),), -0.2, 0.2)), 0.015625, 0.0625),
        "adj_tiles": jnp.clip(1.0 * jax.random.uniform(seeds[2], (N_ROW, N_COL, TILES, TB, TB), jnp.float32) ** level_of(seeds[2], (N_ROW, N_COL, TILES, TB, TB), ((0, 16), (1, 16)), -0.2, 0.2), 0.0, 1.0).astype(jnp.bfloat16),
        "tile_row": place_ends(jax.random.randint(seeds[3], (N_ROW, N_COL, TILES), 0, N_ROW * SUB // TB), jax.random.fold_in(seeds[3], 1), 0, (N_ROW * SUB // TB) - 1).astype(jnp.int32),
        "tile_col": place_ends(jax.random.randint(seeds[4], (N_ROW, N_COL, TILES), 0, N_COL * SUB // TB), jax.random.fold_in(seeds[4], 1), 0, (N_COL * SUB // TB) - 1).astype(jnp.int32),
        "live_count": draw_live_count(jax.random.fold_in(seeds[8], 71), 0),
        "rotation_first": bell_draw(seeds[6], (2 * K, K), (2 * K) ** -0.5, 0.375, (), jnp.float32),
        "rotation_second": bell_draw(seeds[7], (3 * K, K), (3 * K) ** -0.5, 0.3125, (), jnp.float32),
    }


HIGH = lax.Precision.HIGHEST

def apply_operator(block, vertex_scale, adj_tiles, tile_row, tile_col, live_count):
    scaled = (vertex_scale[:, None] * block).astype(jnp.bfloat16)
    panels = scaled.reshape(N_ROW, N_COL * SUB // TB, TB, K)
    row_tiles = N_ROW * SUB // TB
    slot_ids = jnp.arange(TILES, dtype=jnp.int32)

    def device_partial(i, j):
        pieces = panels[i][tile_col[i, j]].astype(jnp.float32)
        tile_out = jnp.einsum('tab,tbk->tak', adj_tiles[i, j].astype(jnp.float32), pieces)
        tile_out = jnp.where((slot_ids < live_count[i, j])[:, None, None], tile_out, 0.0)
        partial_value = jax.ops.segment_sum(tile_out, tile_row[i, j], num_segments=row_tiles)
        partial_value = lax.optimization_barrier(partial_value.reshape(N_ROW, SUB, K).astype(jnp.bfloat16))
        return partial_value.astype(jnp.float32)

    def one_column(j):

        def add_row(i, running):
            return running + device_partial(i, j)
        return lax.fori_loop(0, N_ROW, add_row, jnp.zeros((N_ROW, SUB, K), jnp.float32))
    columns = lax.map(one_column, jnp.arange(N_COL, dtype=jnp.int32))
    summed = jnp.transpose(columns, (1, 0, 2, 3)).reshape(N_ROW * N_COL * SUB, K)
    return block - vertex_scale[:, None] * summed

def residual_block(block, image):
    gram = jnp.dot(block.T, image, precision=HIGH) / VERTS
    resid = image - jnp.dot(block, gram, precision=HIGH)
    colsq = lax.optimization_barrier(jnp.sum(resid * resid, axis=0))
    return resid * lax.rsqrt(colsq / VERTS + 1e-06)

def reference(start_block, vertex_scale, adj_tiles, tile_row, tile_col, live_count, rotation_first, rotation_second):

    def oper(block):
        return apply_operator(block, vertex_scale, adj_tiles, tile_row, tile_col, live_count)
    image0 = oper(start_block)
    search0 = residual_block(start_block, image0)
    simage0 = oper(search0)
    rot_x, rot_w = (rotation_first[:K], rotation_first[K:])
    block1 = jnp.dot(start_block, rot_x, precision=HIGH) + jnp.dot(search0, rot_w, precision=HIGH)
    image1 = jnp.dot(image0, rot_x, precision=HIGH) + jnp.dot(simage0, rot_w, precision=HIGH)
    prev1 = jnp.dot(search0, rot_w, precision=HIGH)
    pimage1 = jnp.dot(simage0, rot_w, precision=HIGH)
    search1 = residual_block(block1, image1)
    simage1 = oper(search1)
    qx, qw, qp = (rotation_second[:K], rotation_second[K:2 * K], rotation_second[2 * K:])
    final_block = jnp.dot(block1, qx, precision=HIGH) + jnp.dot(search1, qw, precision=HIGH) + jnp.dot(prev1, qp, precision=HIGH)
    final_image = jnp.dot(image1, qx, precision=HIGH) + jnp.dot(simage1, qw, precision=HIGH) + jnp.dot(pimage1, qp, precision=HIGH)
    return (final_block, final_image)
```

```python
import jax
import jax.numpy as jnp
from jax import lax
from jax.experimental import pallas as pl
from jax.experimental.pallas import tpu as pltpu
from jax.sharding import PartitionSpec as P

MESH = pl.DeviceIdType.MESH
HIGH = lax.Precision.HIGHEST
F32 = jnp.float32
BF16 = jnp.bfloat16
T = 128
SLOTS = 64
VERTS = 65536
OPS = 3


def mm(left, right):
    return jnp.dot(left, right, precision=HIGH, preferred_element_type=F32)


def gram_of(left, right):
    return lax.dot_general(
        left, right, (((0,), (0,)), ((), ())), precision=HIGH, preferred_element_type=F32
    )


def kernel(
    x_ref, scale_ref, tiles_hbm, rows_ref, cols_ref, live_ref, rot1_ref, rot2_ref,
    block_ref, image_ref,
    tiles, panel_0, panel_1, panel_2, running, index_v, index_s, s_b, d0_ref, x1_ref, d1_ref, p1_ref, dp1_ref, part,
    send_x, send_y, recv_x, recv_y, mid_x, mid_y, last_x, last_y,
    pay, red_a, got_a, red_b, got_s, got_b, got_c,
    tile_sem, index_sem, ag_send, ag_recv, rs_send, rs_recv, ar_send, ar_recv,
):
    panels = (panel_0, panel_1, panel_2)
    r = lax.axis_index("row")
    c = lax.axis_index("col")
    x, y = r // 4, lax.rem(r, 4)
    z, k = c // 2, lax.rem(c, 2)
    sib = c + 1 - 2 * k

    def along_x(step):
        return (lax.rem(x + step, 4) * 4 + y, c)

    def along_y(step):
        return (x * 4 + lax.rem(y + step, 4), c)

    def along_z(step):
        return (r, lax.rem(z + step + 8, 8) * 2 + k)

    def send(src, dst, send_sem, recv_sem, device):
        pltpu.make_async_remote_copy(
            src_ref=src, dst_ref=dst, send_sem=send_sem, recv_sem=recv_sem,
            device_id=device, device_id_type=MESH,
        ).start()

    def wait(ref, sem):
        pltpu.make_async_copy(ref, ref, sem).wait()

    tile_copy = pltpu.make_async_copy(tiles_hbm, tiles, tile_sem)
    tile_copy.start()

    barrier = pltpu.get_barrier_semaphore()

    def greet_row(step, carry):
        pl.semaphore_signal(
            barrier, inc=1, device_id=(lax.rem(r + step, 16), c), device_id_type=MESH
        )
        return carry

    def greet_z(step, carry):
        pl.semaphore_signal(barrier, inc=1, device_id=along_z(step), device_id_type=MESH)
        return carry

    pl.semaphore_signal(barrier, inc=1, device_id=(r, sib), device_id_type=MESH)
    lax.fori_loop(1, 8, greet_z, 0)
    lax.fori_loop(1, 16, greet_row, 0)

    lane = lax.broadcasted_iota(jnp.int32, (T, T), 1)
    sub = lax.broadcasted_iota(jnp.int32, (T, T), 0)
    eye = (lane == sub).astype(F32)
    for half in range(2):
        column = jnp.sum(eye * scale_ref[pl.ds(half, 1), :], axis=1, keepdims=True)
        s_b[pl.ds(half * T, T), :] = jnp.broadcast_to(column, (T, T))

    mine = (k * 8 + z) * 2

    def put_block(op, value):
        scaled = (s_b[...] * value).astype(BF16)
        panels[op][mine] = scaled[:T]
        panels[op][mine + 1] = scaled[T:]

    def at_z(step):
        return (k * 8 + lax.rem(z + step + 8, 8)) * 2

    def gather_start(op):
        own = panels[op].at[pl.ds(mine, 2)]
        send(own, own, ag_send.at[op], ag_recv.at[op, 1], along_z(2))
        send(own, own, ag_send.at[op], ag_recv.at[op, 2], along_z(-2))
        send(own, own, ag_send.at[op], ag_recv.at[op, 3], along_z(1))
        send(own, own, ag_send.at[op], ag_recv.at[op, 4], along_z(-1))
        send(own, own, ag_send.at[op], ag_recv.at[op, 0], (r, sib))

    def to_sibling(op, step):
        block = panels[op].at[pl.ds(at_z(step), 2)]
        send(block, block, ag_send.at[op], ag_recv.at[op, 0], (r, sib))

    def gather_middle(op):
        up = panels[op].at[pl.ds(at_z(-2), 2)]
        low = panels[op].at[pl.ds(at_z(-2), 1)]
        wait(up, ag_recv.at[op, 1])
        send(low, low, ag_send.at[op], ag_recv.at[op, 5], along_z(2))
        send(up, up, ag_send.at[op], ag_recv.at[op, 6], along_z(1))
        down = panels[op].at[pl.ds(at_z(2), 2)]
        high = panels[op].at[pl.ds(at_z(2) + 1, 1)]
        wait(down, ag_recv.at[op, 2])
        send(high, high, ag_send.at[op], ag_recv.at[op, 7], along_z(-2))
        send(down, down, ag_send.at[op], ag_recv.at[op, 8], along_z(-1))
        to_sibling(op, -2)
        to_sibling(op, 2)
        wait(panels[op].at[pl.ds(at_z(-1), 2)], ag_recv.at[op, 3])
        to_sibling(op, -1)
        wait(panels[op].at[pl.ds(at_z(1), 2)], ag_recv.at[op, 4])
        to_sibling(op, 1)

    def gather_end(op):
        wait(panels[op].at[pl.ds(at_z(-3), 2)], ag_recv.at[op, 6])
        to_sibling(op, -3)
        wait(panels[op].at[pl.ds(at_z(3), 2)], ag_recv.at[op, 8])
        to_sibling(op, 3)
        wait(panels[op].at[pl.ds(at_z(4), 1)], ag_recv.at[op, 5])
        wait(panels[op].at[pl.ds(at_z(4) + 1, 1)], ag_recv.at[op, 7])
        to_sibling(op, 4)
        wait(panels[op].at[pl.ds((1 - k) * 16, 16)], ag_recv.at[op, 0])

    def products(op):
        def slot(t, total):
            product = jnp.dot(
                tiles[index_s[0, t]], panels[op][index_s[1, t]], preferred_element_type=F32
            )
            total = jnp.where(index_s[2, t] > 0, product, total + product)
            running[t] = total
            return total

        lax.fori_loop(0, SLOTS, slot, jnp.zeros((T, T), F32), unroll=8)

    def scatter_start(op):
        for step in (1, 3, 2, 0):
            for other in range(4):
                tile = (lax.rem(x + step, 4) * 4 + other) * 2
                send_x[op, step, other] = running[index_s[3, tile]].astype(BF16)
            if step:
                send(send_x.at[op, step], recv_x.at[op, step - 1],
                     rs_send.at[op, 0], rs_recv.at[op, 0], along_x(step))
            for other in range(4):
                tile = (other * 4 + lax.rem(y + step, 4)) * 2 + 1
                send_y[op, step, other] = running[index_s[3, tile]].astype(BF16)
            if step:
                send(send_y.at[op, step], recv_y.at[op, step - 1],
                     rs_send.at[op, 0], rs_recv.at[op, 1], along_y(step))

    def sum_of(own, got, op, at):
        return (
            own[op, 0, at].astype(F32) + got[op, 0, at].astype(F32)
            + got[op, 1, at].astype(F32) + got[op, 2, at].astype(F32)
        )

    def scatter_middle(op):
        wait(recv_x.at[op], rs_recv.at[op, 0])
        for step in (1, 3, 2):
            mid_x[op, step - 1] = sum_of(send_x, recv_x, op, lax.rem(y + step, 4)).astype(BF16)
            send(mid_x.at[op, step - 1], last_x.at[op, step - 1],
                 rs_send.at[op, 1], rs_recv.at[op, 2], along_y(step))
        wait(recv_y.at[op], rs_recv.at[op, 1])
        for step in (1, 3, 2):
            mid_y[op, step - 1] = sum_of(send_y, recv_y, op, lax.rem(x + step, 4)).astype(BF16)
            send(mid_y.at[op, step - 1], last_y.at[op, step - 1],
                 rs_send.at[op, 1], rs_recv.at[op, 3], along_x(step))
        part[pl.ds(0, T), :] = sum_of(send_x, recv_x, op, y)
        part[pl.ds(T, T), :] = sum_of(send_y, recv_y, op, x)

    def scatter_end(op):
        def total(last):
            return (
                last[op, 0].astype(F32) + last[op, 1].astype(F32) + last[op, 2].astype(F32)
            )

        wait(last_x.at[op], rs_recv.at[op, 2])
        part[pl.ds(0, T), :] += total(last_x)
        wait(last_y.at[op], rs_recv.at[op, 3])
        part[pl.ds(T, T), :] += total(last_y)
        return -(s_b[...] * part[...])

    def reduce_start(g, xd, dd):
        pay[g, :, pl.ds(8, 8), :] = xd.reshape(16, 8, T)
        pay[g, :, pl.ds(16, 8), :] = dd.reshape(16, 8, T)

        def one(step, carry):
            to = lax.rem(r + step, 16)
            send(pay.at[g, to], got_a.at[g, step - 1],
                 ar_send.at[g, 0], ar_recv.at[g, 0], (to, c))
            return carry

        lax.fori_loop(1, 16, one, 0)

    def reduce_sibling(g):
        wait(got_a.at[g], ar_recv.at[g, 0])
        red_a[g] = pay[g, r] + jnp.sum(got_a[g], axis=0)
        send(red_a.at[g], got_s.at[g], ar_send.at[g, 1], ar_recv.at[g, 1], (r, sib))

    def reduce_z(g):
        wait(got_s.at[g], ar_recv.at[g, 1])
        red_b[g] = red_a[g] + got_s[g]

        def one(step, carry):
            send(red_b.at[g], got_b.at[g, step - 1],
                 ar_send.at[g, 2], ar_recv.at[g, 2], along_z(step))
            return carry

        lax.fori_loop(1, 8, one, 0)

    def reduce_share(g):
        wait(got_b.at[g], ar_recv.at[g, 2])
        got_c[g, r] = red_b[g] + jnp.sum(got_b[g], axis=0)

        def one(step, carry):
            mine_now = got_c.at[g, r]
            send(mine_now, mine_now, ar_send.at[g, 3], ar_recv.at[g, 3],
                 (lax.rem(r + step, 16), c))
            return carry

        lax.fori_loop(1, 16, one, 0)

    def reduce_end(g):
        wait(got_c.at[g, pl.ds(0, 15)], ar_recv.at[g, 3])
        xs = got_c[g, :, pl.ds(0, 8), :].reshape(T, T)
        xd = got_c[g, :, pl.ds(8, 8), :].reshape(T, T)
        dd = got_c[g, :, pl.ds(16, 8), :].reshape(T, T)
        h = (xs + xd) * (1.0 / VERTS) - eye
        terms = dd - 2.0 * (h * xd) + h * mm(xs, h)
        colsq = jnp.maximum(jnp.sum(terms, axis=0, keepdims=True), 0.0)
        scale = lax.rsqrt(colsq * (1.0 / VERTS) + 1e-06)
        return h, jnp.sum(eye * scale, axis=1, keepdims=True)

    def squares(value):
        square = value * value
        return square[:T] + square[T:]

    def order_slots():
        slots = lax.broadcasted_iota(jnp.int32, (1, T), 1)
        alive = slots < live_ref[0, 0]
        row = jnp.where(alive, rows_ref[...], 32)
        key = row * T + slots

        def column(value):
            spread = jnp.where(lane == sub, jnp.broadcast_to(value, (T, T)), 0)
            return jnp.sum(spread, axis=1, keepdims=True)

        def count(mask, axis):
            return jnp.sum(mask.astype(jnp.int32), axis=axis, keepdims=True)

        row_c, key_c, col_c = column(row), column(key), column(cols_ref[...])
        rank = count(jnp.broadcast_to(key, (T, T)) < key_c, 1)
        below = count(jnp.broadcast_to(row, (T, T)) < row_c, 1)
        here = (rank == lane).astype(jnp.int32)
        place = (col_c // 2 % 2) * 16 + (col_c // 4) * 2 + col_c % 2
        slot_of = jnp.sum(here * sub, axis=0, keepdims=True)
        place_of = jnp.sum(here * place, axis=0, keepdims=True)
        first_of = jnp.sum(here * below, axis=0, keepdims=True) == slots
        upto = count(row_c <= lane, 0)
        same = count(row_c == lane, 0)
        index_v[0:1, :] = jnp.minimum(slot_of, SLOTS - 1)
        index_v[1:2, :] = place_of
        index_v[2:3, :] = first_of.astype(jnp.int32)
        index_v[3:4, :] = jnp.where(same > 0, upto - 1, SLOTS)
        copy = pltpu.make_async_copy(index_v, index_s, index_sem)
        copy.start()
        copy.wait()

    x0 = x_ref[...]
    put_block(0, x0)
    pl.semaphore_wait(barrier, 23)

    gather_start(0)
    order_slots()
    running[SLOTS] = jnp.zeros((T, T), F32)
    gather_middle(0)
    pay[0, :, pl.ds(0, 8), :] = gram_of(x_ref[...], x_ref[...]).reshape(16, 8, T)
    tile_copy.wait()
    gather_end(0)
    products(0)
    scatter_start(0)
    scatter_middle(0)
    d0_ref[...] = scatter_end(0)

    put_block(1, d0_ref[...])
    gather_start(1)
    d0 = d0_ref[...]
    reduce_start(0, gram_of(x_ref[...], d0), squares(d0))
    gather_middle(1)
    reduce_sibling(0)
    gather_end(1)
    reduce_z(0)
    products(1)
    reduce_share(0)
    scatter_start(1)
    scatter_middle(1)
    h0, n0 = reduce_end(0)
    g1 = n0 * rot1_ref[pl.ds(T, T), :]
    h0g1 = mm(h0, g1)
    g2 = rot1_ref[pl.ds(0, T), :] - h0g1
    p1_ref[...] = mm(d0_ref[...], g1) - mm(x_ref[...], h0g1)
    x1_ref[...] = mm(x_ref[...], rot1_ref[pl.ds(0, T), :]) + p1_ref[...]
    dp1_ref[...] = -mm(d0_ref[...], h0g1)
    d1_ref[...] = mm(d0_ref[...], rot1_ref[pl.ds(0, T), :])
    u0g1 = mm(scatter_end(1), g1)
    dp1 = dp1_ref[...] + u0g1
    d1 = d1_ref[...] + dp1
    put_block(2, d1)

    gather_start(2)
    dp1_ref[...] = dp1
    d1_ref[...] = d1
    x1 = x1_ref[...]
    pay[1, :, pl.ds(0, 8), :] = gram_of(x1, x1).reshape(16, 8, T)
    reduce_start(1, gram_of(x1, d1_ref[...]), squares(d1_ref[...]))
    gather_middle(2)
    reduce_sibling(1)
    gather_end(2)
    reduce_z(1)
    products(2)
    reduce_share(1)
    scatter_start(2)
    scatter_middle(2)
    h1, n1 = reduce_end(1)
    q1 = n1 * rot2_ref[pl.ds(T, T), :]
    q2 = rot2_ref[pl.ds(0, T), :] - mm(h1, q1)
    qp = rot2_ref[pl.ds(2 * T, T), :]
    block = mm(x1_ref[...], q2) + mm(d1_ref[...], q1) + mm(p1_ref[...], qp)
    block_ref[...] = block
    image_ref[...] = mm(d1_ref[...], q2) + mm(dp1_ref[...], qp)
    image_ref[...] += block_ref[...] + mm(scatter_end(2), q1)

    for op in range(OPS):
        wait(panels[op].at[pl.ds(0, 30)], ag_send.at[op])
        wait(panels[op].at[pl.ds(0, 24)], rs_send.at[op, 0])
        wait(panels[op].at[pl.ds(0, 6)], rs_send.at[op, 1])
    for g in range(2):
        wait(got_a.at[g], ar_send.at[g, 0])
        wait(got_s.at[g], ar_send.at[g, 1])
        wait(got_b.at[g], ar_send.at[g, 2])
        wait(got_c.at[g, pl.ds(0, 15)], ar_send.at[g, 3])


def local(
    start_block, vertex_scale, adj_tiles, tile_row, tile_col, live_count,
    rotation_first, rotation_second,
):
    pad = ((0, 0), (0, T - SLOTS))
    vmem = pl.BlockSpec(memory_space=pltpu.VMEM)
    tile = (T, T)
    out = jax.ShapeDtypeStruct((2 * T, T), F32)
    dma = pltpu.SemaphoreType.DMA
    return pl.pallas_call(
        kernel,
        out_shape=(out, out),
        in_specs=[
            vmem, vmem, pl.BlockSpec(memory_space=pl.ANY), vmem, vmem,
            pl.BlockSpec(memory_space=pltpu.SMEM), vmem, vmem,
        ],
        out_specs=(vmem, vmem),
        scratch_shapes=[
            pltpu.VMEM((SLOTS, *tile), BF16),
            pltpu.VMEM((32, *tile), BF16),
            pltpu.VMEM((32, *tile), BF16),
            pltpu.VMEM((32, *tile), BF16),
            pltpu.VMEM((SLOTS + 1, *tile), F32),
            pltpu.VMEM((8, T), jnp.int32),
            pltpu.SMEM((8, T), jnp.int32),
        ]
        + [pltpu.VMEM((2 * T, T), F32)] * 7
        + [
            pltpu.VMEM((OPS, 4, 4, *tile), BF16),
            pltpu.VMEM((OPS, 4, 4, *tile), BF16),
            pltpu.VMEM((OPS, 3, 4, *tile), BF16),
            pltpu.VMEM((OPS, 3, 4, *tile), BF16),
        ]
        + [pltpu.VMEM((OPS, 3, *tile), BF16)] * 4
        + [
            pltpu.VMEM((2, 16, 24, T), F32),
            pltpu.VMEM((2, 24, T), F32),
            pltpu.VMEM((2, 15, 24, T), F32),
            pltpu.VMEM((2, 24, T), F32),
            pltpu.VMEM((2, 24, T), F32),
            pltpu.VMEM((2, 7, 24, T), F32),
            pltpu.VMEM((2, 16, 24, T), F32),
            dma,
            dma,
            dma((OPS,)),
            dma((OPS, 9)),
            dma((OPS, 2)),
            dma((OPS, 4)),
            dma((2, 4)),
            dma((2, 4)),
        ],
        compiler_params=pltpu.CompilerParams(
            collective_id=0, has_side_effects=True, vmem_limit_bytes=48 << 20
        ),
        name="lobpcg",
    )(
        start_block,
        vertex_scale.reshape(2, T),
        adj_tiles[0, 0],
        jnp.pad(tile_row[0], pad),
        jnp.pad(tile_col[0], pad),
        live_count,
        rotation_first,
        rotation_second,
    )


def solution(mesh):
    placed = (
        P(("row", "col"), None),
        P(("row", "col")),
        P("row", "col", None, None, None),
        P("row", "col", None),
        P("row", "col", None),
        P("row", "col"),
        P(),
        P(),
    )
    return jax.shard_map(
        local,
        mesh=mesh,
        in_specs=placed,
        out_specs=(P(("row", "col"), None), P(("row", "col"), None)),
        check_vma=False,
    )
```

```python
import jax
import jax.numpy as jnp
from jax import lax
from jax.experimental import pallas as pl
from jax.experimental.pallas import tpu as pltpu
from jax.sharding import PartitionSpec as P

MESH = pl.DeviceIdType.MESH
HIGH = lax.Precision.HIGHEST
F32 = jnp.float32
BF16 = jnp.bfloat16
T = 128
SLOTS = 64
VERTS = 65536
OPS = 3


def mm(left, right):
    return jnp.dot(left, right, precision=HIGH, preferred_element_type=F32)


def gram_of(left, right):
    return lax.dot_general(
        left, right, (((0,), (0,)), ((), ())), precision=HIGH, preferred_element_type=F32
    )


def kernel(
    x_hbm, scale_hbm, tiles_hbm, rows_hbm, cols_hbm, live_hbm, rot1_hbm, rot2_hbm,
    block_ref, image_ref,
    x_ref, scale_ref, rows_ref, cols_ref, live_ref, rot1_ref, rot2_ref,
    tiles, panel_0, panel_1, panel_2, running, index_v, index_s, s_b, d0_ref, u0_ref, g1_ref, g2_ref, x1_ref, d1_ref, p1_ref, dp1_ref, part,
    send_x, send_y, recv_x, recv_y, mid_x, mid_y, last_x, last_y,
    pay, red_a, got_a, red_b, got_s, got_b, got_c,
    in_sem, index_sem, ag_send, ag_recv, rs_send, rs_recv, ar_send, ar_recv,
):
    panels = (panel_0, panel_1, panel_2)
    r = lax.axis_index("row")
    c = lax.axis_index("col")
    x, y = r // 4, lax.rem(r, 4)
    z, k = c // 2, lax.rem(c, 2)
    sib = c + 1 - 2 * k

    def along_x(step):
        return (lax.rem(x + step, 4) * 4 + y, c)

    def along_y(step):
        return (x * 4 + lax.rem(y + step, 4), c)

    def along_z(step):
        return (r, lax.rem(z + step + 8, 8) * 2 + k)

    def send(src, dst, send_sem, recv_sem, device):
        pltpu.make_async_remote_copy(
            src_ref=src, dst_ref=dst, send_sem=send_sem, recv_sem=recv_sem,
            device_id=device, device_id_type=MESH,
        ).start()

    def wait(ref, sem):
        pltpu.make_async_copy(ref, ref, sem).wait()

    loads = [
        pltpu.make_async_copy(source, target, in_sem.at[at])
        for at, (source, target) in enumerate((
            (x_hbm, x_ref), (scale_hbm, scale_ref), (rows_hbm, rows_ref), (cols_hbm, cols_ref),
            (tiles_hbm, tiles), (rot1_hbm, rot1_ref), (rot2_hbm, rot2_ref), (live_hbm, live_ref),
        ))
    ]
    for load in loads:
        load.start()

    barrier = pltpu.get_barrier_semaphore()

    def greet_row(step, carry):
        pl.semaphore_signal(
            barrier, inc=1, device_id=(lax.rem(r + step, 16), c), device_id_type=MESH
        )
        return carry

    def greet_z(step, carry):
        pl.semaphore_signal(barrier, inc=1, device_id=along_z(step), device_id_type=MESH)
        return carry

    pl.semaphore_signal(barrier, inc=1, device_id=(r, sib), device_id_type=MESH)
    lax.fori_loop(1, 8, greet_z, 0)
    lax.fori_loop(1, 16, greet_row, 0)

    lane = lax.broadcasted_iota(jnp.int32, (T, T), 1)
    sub = lax.broadcasted_iota(jnp.int32, (T, T), 0)
    eye = (lane == sub).astype(F32)
    loads[1].wait()
    for half in range(2):
        column = jnp.sum(eye * scale_ref[pl.ds(half, 1), :], axis=1, keepdims=True)
        s_b[pl.ds(half * T, T), :] = jnp.broadcast_to(column, (T, T))

    mine = (k * 8 + z) * 2

    def put_block(op, value):
        scaled = (s_b[...] * value).astype(BF16)
        panels[op][mine] = scaled[:T]
        panels[op][mine + 1] = scaled[T:]

    def at_z(step):
        return (k * 8 + lax.rem(z + step + 8, 8)) * 2

    def gather_start(op):
        own = panels[op].at[pl.ds(mine, 2)]
        send(own, own, ag_send.at[op], ag_recv.at[op, 1], along_z(2))
        send(own, own, ag_send.at[op], ag_recv.at[op, 2], along_z(-2))
        send(own, own, ag_send.at[op], ag_recv.at[op, 3], along_z(1))
        send(own, own, ag_send.at[op], ag_recv.at[op, 4], along_z(-1))
        send(own, own, ag_send.at[op], ag_recv.at[op, 0], (r, sib))

    def to_sibling(op, step):
        block = panels[op].at[pl.ds(at_z(step), 2)]
        send(block, block, ag_send.at[op], ag_recv.at[op, 0], (r, sib))

    def gather_middle(op):
        up = panels[op].at[pl.ds(at_z(-2), 2)]
        low = panels[op].at[pl.ds(at_z(-2), 1)]
        wait(up, ag_recv.at[op, 1])
        send(low, low, ag_send.at[op], ag_recv.at[op, 5], along_z(2))
        send(up, up, ag_send.at[op], ag_recv.at[op, 6], along_z(1))
        down = panels[op].at[pl.ds(at_z(2), 2)]
        high = panels[op].at[pl.ds(at_z(2) + 1, 1)]
        wait(down, ag_recv.at[op, 2])
        send(high, high, ag_send.at[op], ag_recv.at[op, 7], along_z(-2))
        send(down, down, ag_send.at[op], ag_recv.at[op, 8], along_z(-1))
        to_sibling(op, -2)
        to_sibling(op, 2)
        wait(panels[op].at[pl.ds(at_z(-1), 2)], ag_recv.at[op, 3])
        to_sibling(op, -1)
        wait(panels[op].at[pl.ds(at_z(1), 2)], ag_recv.at[op, 4])
        to_sibling(op, 1)

    def gather_end(op):
        wait(panels[op].at[pl.ds(at_z(-3), 2)], ag_recv.at[op, 6])
        to_sibling(op, -3)
        wait(panels[op].at[pl.ds(at_z(3), 2)], ag_recv.at[op, 8])
        to_sibling(op, 3)
        wait(panels[op].at[pl.ds(at_z(4), 1)], ag_recv.at[op, 5])
        wait(panels[op].at[pl.ds(at_z(4) + 1, 1)], ag_recv.at[op, 7])
        to_sibling(op, 4)
        wait(panels[op].at[pl.ds((1 - k) * 16, 16)], ag_recv.at[op, 0])

    def products(op):
        def slot(t, total):
            product = jnp.dot(
                tiles[index_s[0, t]], panels[op][index_s[1, t]], preferred_element_type=F32
            )
            total = jnp.where(index_s[2, t] > 0, product, total + product)
            running[t] = total
            return total

        lax.fori_loop(0, SLOTS, slot, jnp.zeros((T, T), F32), unroll=8)

    def scatter_start(op):
        for step in (1, 3, 2, 0):
            for other in range(4):
                tile = (lax.rem(x + step, 4) * 4 + other) * 2
                send_x[op, step, other] = running[index_s[3, tile]].astype(BF16)
            if step:
                send(send_x.at[op, step], recv_x.at[op, step - 1],
                     rs_send.at[op, 0], rs_recv.at[op, 0], along_x(step))
            for other in range(4):
                tile = (other * 4 + lax.rem(y + step, 4)) * 2 + 1
                send_y[op, step, other] = running[index_s[3, tile]].astype(BF16)
            if step:
                send(send_y.at[op, step], recv_y.at[op, step - 1],
                     rs_send.at[op, 0], rs_recv.at[op, 1], along_y(step))

    def sum_of(own, got, op, at):
        return (
            own[op, 0, at].astype(F32) + got[op, 0, at].astype(F32)
            + got[op, 1, at].astype(F32) + got[op, 2, at].astype(F32)
        )

    def scatter_middle(op):
        wait(recv_x.at[op], rs_recv.at[op, 0])
        for step in (1, 3, 2):
            mid_x[op, step - 1] = sum_of(send_x, recv_x, op, lax.rem(y + step, 4)).astype(BF16)
            send(mid_x.at[op, step - 1], last_x.at[op, step - 1],
                 rs_send.at[op, 1], rs_recv.at[op, 2], along_y(step))
        wait(recv_y.at[op], rs_recv.at[op, 1])
        for step in (1, 3, 2):
            mid_y[op, step - 1] = sum_of(send_y, recv_y, op, lax.rem(x + step, 4)).astype(BF16)
            send(mid_y.at[op, step - 1], last_y.at[op, step - 1],
                 rs_send.at[op, 1], rs_recv.at[op, 3], along_x(step))
        part[pl.ds(0, T), :] = sum_of(send_x, recv_x, op, y)
        part[pl.ds(T, T), :] = sum_of(send_y, recv_y, op, x)

    def scatter_end(op):
        def total(last):
            return (
                last[op, 0].astype(F32) + last[op, 1].astype(F32) + last[op, 2].astype(F32)
            )

        wait(last_x.at[op], rs_recv.at[op, 2])
        part[pl.ds(0, T), :] += total(last_x)
        wait(last_y.at[op], rs_recv.at[op, 3])
        part[pl.ds(T, T), :] += total(last_y)
        return -(s_b[...] * part[...])

    def reduce_start(g, xd, dd):
        pay[g, :, pl.ds(8, 8), :] = xd.reshape(16, 8, T)
        pay[g, :, pl.ds(16, 8), :] = dd.reshape(16, 8, T)

        def one(step, carry):
            to = lax.rem(r + step, 16)
            send(pay.at[g, to], got_a.at[g, step - 1],
                 ar_send.at[g, 0], ar_recv.at[g, 0], (to, c))
            return carry

        lax.fori_loop(1, 16, one, 0)

    def reduce_sibling(g):
        wait(got_a.at[g], ar_recv.at[g, 0])
        red_a[g] = pay[g, r] + jnp.sum(got_a[g], axis=0)
        send(red_a.at[g], got_s.at[g], ar_send.at[g, 1], ar_recv.at[g, 1], (r, sib))

    def reduce_z(g):
        wait(got_s.at[g], ar_recv.at[g, 1])
        red_b[g] = red_a[g] + got_s[g]

        def one(step, carry):
            send(red_b.at[g], got_b.at[g, step - 1],
                 ar_send.at[g, 2], ar_recv.at[g, 2], along_z(step))
            return carry

        lax.fori_loop(1, 8, one, 0)

    def reduce_share(g):
        wait(got_b.at[g], ar_recv.at[g, 2])
        got_c[g, r] = red_b[g] + jnp.sum(got_b[g], axis=0)

        def one(step, carry):
            mine_now = got_c.at[g, r]
            send(mine_now, mine_now, ar_send.at[g, 3], ar_recv.at[g, 3],
                 (lax.rem(r + step, 16), c))
            return carry

        lax.fori_loop(1, 16, one, 0)

    def reduce_end(g):
        wait(got_c.at[g, pl.ds(0, 15)], ar_recv.at[g, 3])
        xs = got_c[g, :, pl.ds(0, 8), :].reshape(T, T)
        xd = got_c[g, :, pl.ds(8, 8), :].reshape(T, T)
        dd = got_c[g, :, pl.ds(16, 8), :].reshape(T, T)
        h = (xs + xd) * (1.0 / VERTS) - eye
        terms = dd - 2.0 * (h * xd) + h * mm(xs, h)
        colsq = jnp.maximum(jnp.sum(terms, axis=0, keepdims=True), 0.0)
        scale = lax.rsqrt(colsq * (1.0 / VERTS) + 1e-06)
        return h, jnp.sum(eye * scale, axis=1, keepdims=True)

    def squares(value):
        square = value * value
        return square[:T] + square[T:]

    def order_slots():
        wide = (SLOTS, SLOTS)
        slots = lax.broadcasted_iota(jnp.int32, (1, SLOTS), 1)
        at_lane = lax.broadcasted_iota(jnp.int32, wide, 1)
        at_sub = lax.broadcasted_iota(jnp.int32, wide, 0)
        row = jnp.where(slots < live_ref[0, 0], rows_ref[...], 32)
        key = row * SLOTS + slots

        def column(value):
            spread = jnp.where(at_lane == at_sub, jnp.broadcast_to(value, wide), 0)
            return jnp.sum(spread, axis=1, keepdims=True)

        def count(mask, axis):
            return jnp.sum(mask.astype(jnp.int32), axis=axis, keepdims=True)

        row_c, key_c, col_c = column(row), column(key), column(cols_ref[...])
        rank = count(jnp.broadcast_to(key, wide) < key_c, 1)
        below = count(jnp.broadcast_to(row, wide) < row_c, 1)
        here = (rank == at_lane).astype(jnp.int32)
        place = (col_c // 2 % 2) * 16 + (col_c // 4) * 2 + col_c % 2
        first_of = jnp.sum(here * below, axis=0, keepdims=True) == slots
        upto = count(row_c <= at_lane, 0)
        same = count(row_c == at_lane, 0)
        index_v[0:1, :] = jnp.sum(here * at_sub, axis=0, keepdims=True)
        index_v[1:2, :] = jnp.sum(here * place, axis=0, keepdims=True)
        index_v[2:3, :] = first_of.astype(jnp.int32)
        index_v[3:4, :] = jnp.where(same > 0, upto - 1, SLOTS)
        copy = pltpu.make_async_copy(index_v, index_s, index_sem)
        copy.start()
        copy.wait()

    loads[0].wait()
    x0 = x_ref[...]
    put_block(0, x0)
    pl.semaphore_wait(barrier, 23)

    gather_start(0)
    loads[2].wait()
    loads[3].wait()
    loads[7].wait()
    order_slots()
    loads[5].wait()
    loads[6].wait()
    running[SLOTS] = jnp.zeros((T, T), F32)
    gather_middle(0)
    pay[0, :, pl.ds(0, 8), :] = gram_of(x_ref[...], x_ref[...]).reshape(16, 8, T)
    loads[4].wait()
    gather_end(0)
    products(0)
    scatter_start(0)
    scatter_middle(0)
    d0_ref[...] = scatter_end(0)

    put_block(1, d0_ref[...])
    gather_start(1)
    d0 = d0_ref[...]
    reduce_start(0, gram_of(x_ref[...], d0), squares(d0))
    gather_middle(1)
    reduce_sibling(0)
    gather_end(1)
    products(1)
    scatter_start(1)
    reduce_z(0)
    scatter_middle(1)
    reduce_share(0)
    u0_ref[...] = scatter_end(1)

    put_block(2, u0_ref[...])
    gather_start(2)
    h0, n0 = reduce_end(0)
    g1 = n0 * rot1_ref[pl.ds(T, T), :]
    h0g1 = mm(h0, g1)
    g1_ref[...] = g1
    g2_ref[...] = rot1_ref[pl.ds(0, T), :] - h0g1
    p1_ref[...] = mm(d0_ref[...], g1)
    p1_ref[...] -= mm(x_ref[...], h0g1)
    dp1_ref[...] = mm(u0_ref[...], g1)
    dp1_ref[...] -= mm(d0_ref[...], h0g1)
    gather_middle(2)
    x1_ref[...] = mm(x_ref[...], rot1_ref[pl.ds(0, T), :]) + p1_ref[...]
    d1_ref[...] = mm(d0_ref[...], rot1_ref[pl.ds(0, T), :]) + dp1_ref[...]
    x1 = x1_ref[...]
    pay[1, :, pl.ds(0, 8), :] = gram_of(x1, x1).reshape(16, 8, T)
    reduce_start(1, gram_of(x1, d1_ref[...]), squares(d1_ref[...]))
    gather_end(2)
    products(2)
    scatter_start(2)
    reduce_sibling(1)
    reduce_z(1)
    scatter_middle(2)
    reduce_share(1)
    qp = rot2_ref[pl.ds(2 * T, T), :]
    block_ref[...] = mm(p1_ref[...], qp)
    image_ref[...] = mm(dp1_ref[...], qp)
    h1, n1 = reduce_end(1)
    q1 = n1 * rot2_ref[pl.ds(T, T), :]
    q2 = rot2_ref[pl.ds(0, T), :] - mm(h1, q1)
    block_ref[...] += mm(d1_ref[...], q1)
    block_ref[...] += mm(x1_ref[...], q2)
    image_ref[...] += mm(d1_ref[...], q2)
    image_ref[...] += mm(u0_ref[...], mm(g2_ref[...], q1))
    image_ref[...] += block_ref[...]
    g1q1 = mm(g1_ref[...], q1)
    image_ref[...] += mm(scatter_end(2), g1q1)

    for op in range(OPS):
        wait(panels[op].at[pl.ds(0, 30)], ag_send.at[op])
        wait(panels[op].at[pl.ds(0, 24)], rs_send.at[op, 0])
        wait(panels[op].at[pl.ds(0, 6)], rs_send.at[op, 1])
    for g in range(2):
        wait(got_a.at[g], ar_send.at[g, 0])
        wait(got_s.at[g], ar_send.at[g, 1])
        wait(got_b.at[g], ar_send.at[g, 2])
        wait(got_c.at[g, pl.ds(0, 15)], ar_send.at[g, 3])


def local(
    start_block, vertex_scale, adj_tiles, tile_row, tile_col, live_count,
    rotation_first, rotation_second,
):
    vmem = pl.BlockSpec(memory_space=pltpu.VMEM)
    hbm = pl.BlockSpec(memory_space=pl.ANY)
    tile = (T, T)
    out = jax.ShapeDtypeStruct((2 * T, T), F32)
    dma = pltpu.SemaphoreType.DMA
    return pl.pallas_call(
        kernel,
        out_shape=(out, out),
        in_specs=[hbm] * 8,
        out_specs=(vmem, vmem),
        scratch_shapes=[
            pltpu.VMEM((2 * T, T), F32),
            pltpu.VMEM((2, T), F32),
            pltpu.VMEM((1, SLOTS), jnp.int32),
            pltpu.VMEM((1, SLOTS), jnp.int32),
            pltpu.SMEM((1, 1), jnp.int32),
            pltpu.VMEM((2 * T, T), F32),
            pltpu.VMEM((3 * T, T), F32),
            pltpu.VMEM((SLOTS, *tile), BF16),
            pltpu.VMEM((32, *tile), BF16),
            pltpu.VMEM((32, *tile), BF16),
            pltpu.VMEM((32, *tile), BF16),
            pltpu.VMEM((SLOTS + 1, *tile), F32),
            pltpu.VMEM((8, SLOTS), jnp.int32),
            pltpu.SMEM((8, SLOTS), jnp.int32),
        ]
        + [pltpu.VMEM((2 * T, T), F32)] * 3
        + [pltpu.VMEM(tile, F32)] * 2
        + [pltpu.VMEM((2 * T, T), F32)] * 5
        + [
            pltpu.VMEM((OPS, 4, 4, *tile), BF16),
            pltpu.VMEM((OPS, 4, 4, *tile), BF16),
            pltpu.VMEM((OPS, 3, 4, *tile), BF16),
            pltpu.VMEM((OPS, 3, 4, *tile), BF16),
        ]
        + [pltpu.VMEM((OPS, 3, *tile), BF16)] * 4
        + [
            pltpu.VMEM((2, 16, 24, T), F32),
            pltpu.VMEM((2, 24, T), F32),
            pltpu.VMEM((2, 15, 24, T), F32),
            pltpu.VMEM((2, 24, T), F32),
            pltpu.VMEM((2, 24, T), F32),
            pltpu.VMEM((2, 7, 24, T), F32),
            pltpu.VMEM((2, 16, 24, T), F32),
            dma((8,)),
            dma,
            dma((OPS,)),
            dma((OPS, 9)),
            dma((OPS, 2)),
            dma((OPS, 4)),
            dma((2, 4)),
            dma((2, 4)),
        ],
        compiler_params=pltpu.CompilerParams(
            collective_id=0, has_side_effects=True, vmem_limit_bytes=60 << 20
        ),
        name="lobpcg",
    )(
        start_block,
        vertex_scale.reshape(2, T),
        adj_tiles[0, 0],
        tile_row[0],
        tile_col[0],
        live_count,
        rotation_first,
        rotation_second,
    )


def solution(mesh):
    placed = (
        P(("row", "col"), None),
        P(("row", "col")),
        P("row", "col", None, None, None),
        P("row", "col", None),
        P("row", "col", None),
        P("row", "col"),
        P(),
        P(),
    )
    return jax.shard_map(
        local,
        mesh=mesh,
        in_specs=placed,
        out_specs=(P(("row", "col"), None), P(("row", "col"), None)),
        check_vma=False,
    )
```

```python
import jax
import jax.numpy as jnp
from jax import lax
from jax.experimental import pallas as pl
from jax.experimental.pallas import tpu as pltpu
from jax.sharding import PartitionSpec as P

MESH = pl.DeviceIdType.MESH
HIGH = lax.Precision.HIGHEST
F32 = jnp.float32
BF16 = jnp.bfloat16
T = 128
SLOTS = 64
VERTS = 65536
HALF = 64
CHAINS = 6


def mm(left, right):
    return jnp.dot(left, right, precision=HIGH, preferred_element_type=F32)


def gram_of(left, right):
    return lax.dot_general(
        left, right, (((0,), (0,)), ((), ())), precision=HIGH, preferred_element_type=F32
    )


def kernel(
    x_hbm, scale_hbm, tiles_hbm, rows_hbm, cols_hbm, live_hbm, rot1_hbm, rot2_hbm,
    block_ref, image_ref,
    x_ref, scale_ref, rows_ref, cols_ref, live_ref, rot1_ref, rot2_ref,
    tiles, panel_0, panel_1, panel_2, panel_3, panel_4, panel_5, both, running, index_v, index_s, s_b, held, d0_ref, u0_ref, g1_ref, g2_ref, x1_ref, d1_ref, p1_ref, dp1_ref, part,
    send_x, send_y, recv_x, recv_y, mid_x, mid_y, last_x, last_y,
    pay, red_a, got_a, red_b, got_s, got_b, got_c,
    in_sem, index_sem, ag_send, ag_recv, rs_send, rs_recv, ar_send, ar_recv,
):
    panels = (panel_0, panel_1, panel_2, panel_3, panel_4, panel_5)
    r = lax.axis_index("row")
    c = lax.axis_index("col")
    x, y = r // 4, lax.rem(r, 4)
    z, k = c // 2, lax.rem(c, 2)
    sib = c + 1 - 2 * k

    def along_x(step):
        return (lax.rem(x + step, 4) * 4 + y, c)

    def along_y(step):
        return (x * 4 + lax.rem(y + step, 4), c)

    def along_z(step):
        return (r, lax.rem(z + step + 8, 8) * 2 + k)

    def send(src, dst, send_sem, recv_sem, device):
        pltpu.make_async_remote_copy(
            src_ref=src, dst_ref=dst, send_sem=send_sem, recv_sem=recv_sem,
            device_id=device, device_id_type=MESH,
        ).start()

    def wait(ref, sem):
        pltpu.make_async_copy(ref, ref, sem).wait()

    loads = [
        pltpu.make_async_copy(source, target, in_sem.at[at])
        for at, (source, target) in enumerate((
            (x_hbm, x_ref), (scale_hbm, scale_ref), (rows_hbm, rows_ref), (cols_hbm, cols_ref),
            (tiles_hbm, tiles), (rot1_hbm, rot1_ref), (rot2_hbm, rot2_ref), (live_hbm, live_ref),
        ))
    ]
    for load in loads:
        load.start()

    barrier = pltpu.get_barrier_semaphore()

    def greet_row(step, carry):
        pl.semaphore_signal(
            barrier, inc=1, device_id=(lax.rem(r + step, 16), c), device_id_type=MESH
        )
        return carry

    def greet_z(step, carry):
        pl.semaphore_signal(barrier, inc=1, device_id=along_z(step), device_id_type=MESH)
        return carry

    pl.semaphore_signal(barrier, inc=1, device_id=(r, sib), device_id_type=MESH)
    lax.fori_loop(1, 8, greet_z, 0)
    lax.fori_loop(1, 16, greet_row, 0)

    lane = lax.broadcasted_iota(jnp.int32, (T, T), 1)
    sub = lax.broadcasted_iota(jnp.int32, (T, T), 0)
    eye = (lane == sub).astype(F32)
    loads[1].wait()
    low = lane < HALF

    def turn(value):
        return pltpu.roll(value, HALF, 1)

    def scale_column(half):
        return jnp.sum(eye * scale_ref[pl.ds(half, 1), :], axis=1, keepdims=True)

    s_b[...] = jnp.where(low, scale_column(0), scale_column(1))

    def pack(top, bottom):
        return jnp.where(low, top, turn(bottom)), jnp.where(low, turn(top), bottom)

    def unpack(first, second, target):
        target[pl.ds(0, T), :] = jnp.where(low, first, turn(second))
        target[pl.ds(T, T), :] = jnp.where(low, turn(first), second)

    def at_z(step):
        return k * 8 + lax.rem(z + step + 8, 8)

    def put_block(q, value):
        panels[q][at_z(0)] = (s_b[...] * value).astype(BF16)

    def gather_start(q):
        own = panels[q].at[at_z(0)]
        send(own, own, ag_send.at[q], ag_recv.at[q, 1], along_z(2))
        send(own, own, ag_send.at[q], ag_recv.at[q, 2], along_z(-2))
        send(own, own, ag_send.at[q], ag_recv.at[q, 3], along_z(1))
        send(own, own, ag_send.at[q], ag_recv.at[q, 4], along_z(-1))
        send(own, own, ag_send.at[q], ag_recv.at[q, 0], (r, sib))

    def to_sibling(q, step):
        block = panels[q].at[at_z(step)]
        send(block, block, ag_send.at[q], ag_recv.at[q, 0], (r, sib))

    def gather_middle(q):
        up = panels[q].at[at_z(-2)]
        upper = panels[q].at[at_z(-2), pl.ds(0, HALF)]
        wait(up, ag_recv.at[q, 1])
        send(upper, upper, ag_send.at[q], ag_recv.at[q, 5], along_z(2))
        send(up, up, ag_send.at[q], ag_recv.at[q, 6], along_z(1))
        down = panels[q].at[at_z(2)]
        lower = panels[q].at[at_z(2), pl.ds(HALF, HALF)]
        wait(down, ag_recv.at[q, 2])
        send(lower, lower, ag_send.at[q], ag_recv.at[q, 7], along_z(-2))
        send(down, down, ag_send.at[q], ag_recv.at[q, 8], along_z(-1))
        to_sibling(q, -2)
        to_sibling(q, 2)
        wait(panels[q].at[at_z(-1)], ag_recv.at[q, 3])
        to_sibling(q, -1)
        wait(panels[q].at[at_z(1)], ag_recv.at[q, 4])
        to_sibling(q, 1)

    def spread(q, core):
        def one(at, carry):
            block = panels[q][core * 8 + at]
            both[core * 8 + at] = block
            both[16 + core * 8 + at] = turn(block.astype(F32)).astype(BF16)
            return carry

        lax.fori_loop(0, 8, one, 0, unroll=8)

    def gather_end(q):
        wait(panels[q].at[at_z(-3)], ag_recv.at[q, 6])
        to_sibling(q, -3)
        wait(panels[q].at[at_z(3)], ag_recv.at[q, 8])
        to_sibling(q, 3)
        wait(panels[q].at[at_z(4), pl.ds(0, HALF)], ag_recv.at[q, 5])
        wait(panels[q].at[at_z(4), pl.ds(HALF, HALF)], ag_recv.at[q, 7])
        to_sibling(q, 4)
        spread(q, k)
        wait(panels[q].at[pl.ds((1 - k) * 8, 8)], ag_recv.at[q, 0])
        spread(q, 1 - k)

    def products(q):
        def slot(t, total):
            product = jnp.dot(
                tiles[index_s[0, t]], both[index_s[1, t]], preferred_element_type=F32
            )
            total = jnp.where(index_s[2, t] > 0, product, total + product)
            running[t] = total
            return total

        lax.fori_loop(0, SLOTS, slot, jnp.zeros((T, T), F32), unroll=64)

    def scatter_start(q):
        def rows(to, start):
            return jnp.where(
                low[:HALF],
                running[index_s[3, to * 2], pl.ds(start, HALF)],
                running[index_s[3, to * 2 + 1], pl.ds(start, HALF)],
            ).astype(BF16)

        for step in (1, 3, 2, 0):
            for other in range(4):
                send_x[q, step, other] = rows(lax.rem(x + step, 4) * 4 + other, 0)
            if step:
                send(send_x.at[q, step], recv_x.at[q, step - 1],
                     rs_send.at[q, 0], rs_recv.at[q, 0], along_x(step))
            for other in range(4):
                send_y[q, step, other] = rows(other * 4 + lax.rem(y + step, 4), HALF)
            if step:
                send(send_y.at[q, step], recv_y.at[q, step - 1],
                     rs_send.at[q, 0], rs_recv.at[q, 1], along_y(step))

    def sum_of(own, got, q, at):
        return (
            own[q, 0, at].astype(F32) + got[q, 0, at].astype(F32)
            + got[q, 1, at].astype(F32) + got[q, 2, at].astype(F32)
        )

    def scatter_middle(q):
        wait(recv_x.at[q], rs_recv.at[q, 0])
        for step in (1, 3, 2):
            mid_x[q, step - 1] = sum_of(send_x, recv_x, q, lax.rem(y + step, 4)).astype(BF16)
            send(mid_x.at[q, step - 1], last_x.at[q, step - 1],
                 rs_send.at[q, 1], rs_recv.at[q, 2], along_y(step))
        wait(recv_y.at[q], rs_recv.at[q, 1])
        for step in (1, 3, 2):
            mid_y[q, step - 1] = sum_of(send_y, recv_y, q, lax.rem(x + step, 4)).astype(BF16)
            send(mid_y.at[q, step - 1], last_y.at[q, step - 1],
                 rs_send.at[q, 1], rs_recv.at[q, 3], along_x(step))
        part[q % 2, pl.ds(0, HALF), :] = sum_of(send_x, recv_x, q, y)
        part[q % 2, pl.ds(HALF, HALF), :] = sum_of(send_y, recv_y, q, x)

    def scatter_end(q):
        def total(last):
            return (
                last[q, 0].astype(F32) + last[q, 1].astype(F32) + last[q, 2].astype(F32)
            )

        wait(last_x.at[q], rs_recv.at[q, 2])
        part[q % 2, pl.ds(0, HALF), :] += total(last_x)
        wait(last_y.at[q], rs_recv.at[q, 3])
        part[q % 2, pl.ds(HALF, HALF), :] += total(last_y)
        held[q % 2] = -(s_b[...] * part[q % 2])

    def next_gather(q):
        scatter_end(q)
        put_block(q + 2, held[q % 2])
        gather_start(q + 2)

    def multiply(q):
        gather_end(q)
        products(q)
        scatter_start(q)

    def reduce_start(g, xd, dd):
        pay[g, :, pl.ds(8, 8), :] = xd.reshape(16, 8, T)
        pay[g, :, pl.ds(16, 8), :] = dd.reshape(16, 8, T)

        def one(step, carry):
            to = lax.rem(r + step, 16)
            send(pay.at[g, to], got_a.at[g, step - 1],
                 ar_send.at[g, 0], ar_recv.at[g, 0], (to, c))
            return carry

        lax.fori_loop(1, 16, one, 0)

    def reduce_sibling(g):
        wait(got_a.at[g], ar_recv.at[g, 0])
        red_a[g] = pay[g, r] + jnp.sum(got_a[g], axis=0)
        send(red_a.at[g], got_s.at[g], ar_send.at[g, 1], ar_recv.at[g, 1], (r, sib))

    def reduce_z(g):
        wait(got_s.at[g], ar_recv.at[g, 1])
        red_b[g] = red_a[g] + got_s[g]

        def one(step, carry):
            send(red_b.at[g], got_b.at[g, step - 1],
                 ar_send.at[g, 2], ar_recv.at[g, 2], along_z(step))
            return carry

        lax.fori_loop(1, 8, one, 0)

    def reduce_share(g):
        wait(got_b.at[g], ar_recv.at[g, 2])
        got_c[g, r] = red_b[g] + jnp.sum(got_b[g], axis=0)

        def one(step, carry):
            mine_now = got_c.at[g, r]
            send(mine_now, mine_now, ar_send.at[g, 3], ar_recv.at[g, 3],
                 (lax.rem(r + step, 16), c))
            return carry

        lax.fori_loop(1, 16, one, 0)

    def reduce_end(g):
        wait(got_c.at[g, pl.ds(0, 15)], ar_recv.at[g, 3])
        xs = got_c[g, :, pl.ds(0, 8), :].reshape(T, T)
        xd = got_c[g, :, pl.ds(8, 8), :].reshape(T, T)
        dd = got_c[g, :, pl.ds(16, 8), :].reshape(T, T)
        h = (xs + xd) * (1.0 / VERTS) - eye
        terms = dd - 2.0 * (h * xd) + h * mm(xs, h)
        colsq = jnp.maximum(jnp.sum(terms, axis=0, keepdims=True), 0.0)
        scale = lax.rsqrt(colsq * (1.0 / VERTS) + 1e-06)
        return h, jnp.sum(eye * scale, axis=1, keepdims=True)

    def squares(value):
        square = value * value
        return square[:T] + square[T:]

    def order_slots():
        wide = (SLOTS, SLOTS)
        slots = lax.broadcasted_iota(jnp.int32, (1, SLOTS), 1)
        at_lane = lax.broadcasted_iota(jnp.int32, wide, 1)
        at_sub = lax.broadcasted_iota(jnp.int32, wide, 0)
        row = jnp.where(slots < live_ref[0, 0], rows_ref[...], 32)
        key = row * SLOTS + slots

        def column(value):
            spread = jnp.where(at_lane == at_sub, jnp.broadcast_to(value, wide), 0)
            return jnp.sum(spread, axis=1, keepdims=True)

        def count(mask, axis):
            return jnp.sum(mask.astype(jnp.int32), axis=axis, keepdims=True)

        row_c, key_c, col_c = column(row), column(key), column(cols_ref[...])
        rank = count(jnp.broadcast_to(key, wide) < key_c, 1)
        below = count(jnp.broadcast_to(row, wide) < row_c, 1)
        here = (rank == at_lane).astype(jnp.int32)
        turned = (row_c + col_c) % 2
        place = turned * 16 + (col_c // 2 % 2) * 8 + col_c // 4
        first_of = jnp.sum(here * below, axis=0, keepdims=True) == slots
        upto = count(row_c <= at_lane, 0)
        same = count(row_c == at_lane, 0)
        index_v[0:1, :] = jnp.sum(here * at_sub, axis=0, keepdims=True)
        index_v[1:2, :] = jnp.sum(here * place, axis=0, keepdims=True)
        index_v[2:3, :] = first_of.astype(jnp.int32)
        index_v[3:4, :] = jnp.where(same > 0, upto - 1, SLOTS)
        copy = pltpu.make_async_copy(index_v, index_s, index_sem)
        copy.start()
        copy.wait()

    loads[0].wait()
    for q, value in enumerate(pack(x_ref[pl.ds(0, T), :], x_ref[pl.ds(T, T), :])):
        put_block(q, value)
    pl.semaphore_wait(barrier, 23)

    gather_start(0)
    gather_start(1)
    for load in (2, 3, 7):
        loads[load].wait()
    order_slots()
    running[SLOTS] = jnp.zeros((T, T), F32)
    gather_middle(0)
    gather_middle(1)
    pay[0, :, pl.ds(0, 8), :] = gram_of(x_ref[...], x_ref[...]).reshape(16, 8, T)
    for load in (4, 5, 6):
        loads[load].wait()
    multiply(0)
    multiply(1)
    scatter_middle(0)
    scatter_middle(1)
    next_gather(0)
    next_gather(1)

    unpack(held[0], held[1], d0_ref)
    d0 = d0_ref[...]
    reduce_start(0, gram_of(x_ref[...], d0), squares(d0))
    gather_middle(2)
    gather_middle(3)
    multiply(2)
    reduce_sibling(0)
    multiply(3)
    reduce_z(0)
    scatter_middle(2)
    scatter_middle(3)
    reduce_share(0)
    next_gather(2)
    next_gather(3)

    unpack(held[0], held[1], u0_ref)
    h0, n0 = reduce_end(0)
    g1 = n0 * rot1_ref[pl.ds(T, T), :]
    h0g1 = mm(h0, g1)
    g1_ref[...] = g1
    g2_ref[...] = rot1_ref[pl.ds(0, T), :] - h0g1
    p1_ref[...] = mm(d0_ref[...], g1)
    p1_ref[...] -= mm(x_ref[...], h0g1)
    dp1_ref[...] = mm(u0_ref[...], g1)
    dp1_ref[...] -= mm(d0_ref[...], h0g1)
    gather_middle(4)
    gather_middle(5)
    x1_ref[...] = mm(x_ref[...], rot1_ref[pl.ds(0, T), :]) + p1_ref[...]
    d1_ref[...] = mm(d0_ref[...], rot1_ref[pl.ds(0, T), :]) + dp1_ref[...]
    x1 = x1_ref[...]
    pay[1, :, pl.ds(0, 8), :] = gram_of(x1, x1).reshape(16, 8, T)
    reduce_start(1, gram_of(x1, d1_ref[...]), squares(d1_ref[...]))
    multiply(4)
    reduce_sibling(1)
    multiply(5)
    reduce_z(1)
    scatter_middle(4)
    scatter_middle(5)
    reduce_share(1)
    qp = rot2_ref[pl.ds(2 * T, T), :]
    block_ref[...] = mm(p1_ref[...], qp)
    image_ref[...] = mm(dp1_ref[...], qp)
    h1, n1 = reduce_end(1)
    q1 = n1 * rot2_ref[pl.ds(T, T), :]
    q2 = rot2_ref[pl.ds(0, T), :] - mm(h1, q1)
    block_ref[...] += mm(d1_ref[...], q1)
    block_ref[...] += mm(x1_ref[...], q2)
    image_ref[...] += mm(d1_ref[...], q2)
    image_ref[...] += mm(u0_ref[...], mm(g2_ref[...], q1))
    image_ref[...] += block_ref[...]
    g1_ref[...] = mm(g1_ref[...], q1)
    scatter_end(4)
    scatter_end(5)
    unpack(held[0], held[1], d0_ref)
    image_ref[...] += mm(d0_ref[...], g1_ref[...])

    for q in range(CHAINS):
        wait(both.at[pl.ds(0, 15)], ag_send.at[q])
        wait(both.at[pl.ds(0, 12)], rs_send.at[q, 0])
        wait(both.at[pl.ds(0, 3)], rs_send.at[q, 1])
    for g in range(2):
        wait(got_a.at[g], ar_send.at[g, 0])
        wait(got_s.at[g], ar_send.at[g, 1])
        wait(got_b.at[g], ar_send.at[g, 2])
        wait(got_c.at[g, pl.ds(0, 15)], ar_send.at[g, 3])


def local(
    start_block, vertex_scale, adj_tiles, tile_row, tile_col, live_count,
    rotation_first, rotation_second,
):
    vmem = pl.BlockSpec(memory_space=pltpu.VMEM)
    hbm = pl.BlockSpec(memory_space=pl.ANY)
    tile = (T, T)
    out = jax.ShapeDtypeStruct((2 * T, T), F32)
    dma = pltpu.SemaphoreType.DMA
    return pl.pallas_call(
        kernel,
        out_shape=(out, out),
        in_specs=[hbm] * 8,
        out_specs=(vmem, vmem),
        scratch_shapes=[
            pltpu.VMEM((2 * T, T), F32),
            pltpu.VMEM((2, T), F32),
            pltpu.VMEM((1, SLOTS), jnp.int32),
            pltpu.VMEM((1, SLOTS), jnp.int32),
            pltpu.SMEM((1, 1), jnp.int32),
            pltpu.VMEM((2 * T, T), F32),
            pltpu.VMEM((3 * T, T), F32),
            pltpu.VMEM((SLOTS, *tile), BF16),
        ]
        + [pltpu.VMEM((16, *tile), BF16)] * CHAINS
        + [
            pltpu.VMEM((32, *tile), BF16),
            pltpu.VMEM((SLOTS + 1, *tile), F32),
            pltpu.VMEM((8, SLOTS), jnp.int32),
            pltpu.SMEM((8, SLOTS), jnp.int32),
        ]
        + [pltpu.VMEM(tile, F32), pltpu.VMEM((2, *tile), F32)]
        + [pltpu.VMEM((2 * T, T), F32)] * 2
        + [pltpu.VMEM(tile, F32)] * 2
        + [pltpu.VMEM((2 * T, T), F32)] * 4
        + [pltpu.VMEM((2, *tile), F32)]
        + [pltpu.VMEM((CHAINS, 4, 4, HALF, T), BF16)] * 2
        + [pltpu.VMEM((CHAINS, 3, 4, HALF, T), BF16)] * 2
        + [pltpu.VMEM((CHAINS, 3, HALF, T), BF16)] * 4
        + [
            pltpu.VMEM((2, 16, 24, T), F32),
            pltpu.VMEM((2, 24, T), F32),
            pltpu.VMEM((2, 15, 24, T), F32),
            pltpu.VMEM((2, 24, T), F32),
            pltpu.VMEM((2, 24, T), F32),
            pltpu.VMEM((2, 7, 24, T), F32),
            pltpu.VMEM((2, 16, 24, T), F32),
            dma((8,)),
            dma,
            dma((CHAINS,)),
            dma((CHAINS, 9)),
            dma((CHAINS, 2)),
            dma((CHAINS, 4)),
            dma((2, 4)),
            dma((2, 4)),
        ],
        compiler_params=pltpu.CompilerParams(
            collective_id=0, has_side_effects=True, vmem_limit_bytes=60 << 20
        ),
        name="lobpcg",
    )(
        start_block,
        vertex_scale.reshape(2, T),
        adj_tiles[0, 0],
        tile_row[0],
        tile_col[0],
        live_count,
        rotation_first,
        rotation_second,
    )


def solution(mesh):
    placed = (
        P(("row", "col"), None),
        P(("row", "col")),
        P("row", "col", None, None, None),
        P("row", "col", None),
        P("row", "col", None),
        P("row", "col"),
        P(),
        P(),
    )
    return jax.shard_map(
        local,
        mesh=mesh,
        in_specs=placed,
        out_specs=(P(("row", "col"), None), P(("row", "col"), None)),
        check_vma=False,
    )
```

```python
import jax
import jax.numpy as jnp
from jax import lax
from jax.experimental import pallas as pl
from jax.experimental.pallas import tpu as pltpu
from jax.sharding import PartitionSpec as P

MESH = pl.DeviceIdType.MESH
HIGH = lax.Precision.HIGHEST
F32 = jnp.float32
BF16 = jnp.bfloat16
T = 128
SLOTS = 64
VERTS = 65536
HALF = 64
ROWS = 17
CHAINS = 6


def mm(left, right):
    return jnp.dot(left, right, precision=HIGH, preferred_element_type=F32)


def gram_of(left, right):
    return lax.dot_general(
        left, right, (((0,), (0,)), ((), ())), precision=HIGH, preferred_element_type=F32
    )


def kernel(
    x_hbm, scale_hbm, tiles_hbm, rows_hbm, cols_hbm, live_hbm, rot1_hbm, rot2_hbm,
    block_ref, image_ref,
    x_ref, scale_ref, rows_ref, cols_ref, live_ref, rot1_ref, rot2_ref,
    tiles, panel_0, panel_1, panel_2, panel_3, panel_4, panel_5, both, running, index_v, index_s, s_b, held, basis, next_ref, last_ref, g_ref, q_ref, part,
    send_x, send_y, recv_x, recv_y, mid_x, mid_y, last_x, last_y,
    pay, red_a, got_a, red_b, got_s, got_b, got_c,
    in_sem, index_sem, ag_send, ag_recv, rs_send, rs_recv, ar_send, ar_recv,
):
    panels = (panel_0, panel_1, panel_2, panel_3, panel_4, panel_5)
    r = lax.axis_index("row")
    c = lax.axis_index("col")
    x, y = r // 4, lax.rem(r, 4)
    z, k = c // 2, lax.rem(c, 2)
    sib = c + 1 - 2 * k

    def along_x(step):
        return (lax.rem(x + step, 4) * 4 + y, c)

    def along_y(step):
        return (x * 4 + lax.rem(y + step, 4), c)

    def along_z(step):
        return (r, lax.rem(z + step + 8, 8) * 2 + k)

    def send(src, dst, send_sem, recv_sem, device):
        pltpu.make_async_remote_copy(
            src_ref=src, dst_ref=dst, send_sem=send_sem, recv_sem=recv_sem,
            device_id=device, device_id_type=MESH,
        ).start()

    def wait(ref, sem):
        pltpu.make_async_copy(ref, ref, sem).wait()

    loads = [
        pltpu.make_async_copy(source, target, in_sem.at[at])
        for at, (source, target) in enumerate((
            (x_hbm, x_ref), (scale_hbm, scale_ref), (rows_hbm, rows_ref), (cols_hbm, cols_ref),
            (tiles_hbm, tiles), (rot1_hbm, rot1_ref), (rot2_hbm, rot2_ref), (live_hbm, live_ref),
        ))
    ]
    for load in loads:
        load.start()

    barrier = pltpu.get_barrier_semaphore()

    def greet_row(step, carry):
        pl.semaphore_signal(
            barrier, inc=1, device_id=(lax.rem(r + step, 16), c), device_id_type=MESH
        )
        return carry

    def greet_z(step, carry):
        pl.semaphore_signal(barrier, inc=1, device_id=along_z(step), device_id_type=MESH)
        return carry

    pl.semaphore_signal(barrier, inc=1, device_id=(r, sib), device_id_type=MESH)
    lax.fori_loop(1, 8, greet_z, 0)
    lax.fori_loop(1, 16, greet_row, 0)

    lane = lax.broadcasted_iota(jnp.int32, (T, T), 1)
    sub = lax.broadcasted_iota(jnp.int32, (T, T), 0)
    eye = (lane == sub).astype(F32)
    loads[1].wait()
    low = lane < HALF

    def turn(value):
        return pltpu.roll(value, HALF, 1)

    def scale_column(half):
        return jnp.sum(eye * scale_ref[pl.ds(half, 1), :], axis=1, keepdims=True)

    s_b[...] = jnp.where(low, scale_column(0), scale_column(1))

    def pack(top, bottom):
        return jnp.where(low, top, turn(bottom)), jnp.where(low, turn(top), bottom)

    def unpack(target, at):
        first, second = held[0], held[1]
        target[pl.ds(0, T), pl.ds(at, T)] = jnp.where(low, first, turn(second))
        target[pl.ds(T, T), pl.ds(at, T)] = jnp.where(low, turn(first), second)

    def at_z(step):
        return k * 8 + lax.rem(z + step + 8, 8)

    def put_block(q, value):
        panels[q][at_z(0)] = (s_b[...] * value).astype(BF16)

    def gather_start(q):
        own = panels[q].at[at_z(0)]
        send(own, own, ag_send.at[q], ag_recv.at[q, 1], along_z(2))
        send(own, own, ag_send.at[q], ag_recv.at[q, 2], along_z(-2))
        send(own, own, ag_send.at[q], ag_recv.at[q, 3], along_z(1))
        send(own, own, ag_send.at[q], ag_recv.at[q, 4], along_z(-1))
        send(own, own, ag_send.at[q], ag_recv.at[q, 0], (r, sib))

    def to_sibling(q, step):
        block = panels[q].at[at_z(step)]
        send(block, block, ag_send.at[q], ag_recv.at[q, 0], (r, sib))

    def gather_middle(q):
        up = panels[q].at[at_z(-2)]
        upper = panels[q].at[at_z(-2), pl.ds(0, HALF)]
        wait(up, ag_recv.at[q, 1])
        send(upper, upper, ag_send.at[q], ag_recv.at[q, 5], along_z(2))
        send(up, up, ag_send.at[q], ag_recv.at[q, 6], along_z(1))
        down = panels[q].at[at_z(2)]
        lower = panels[q].at[at_z(2), pl.ds(HALF, HALF)]
        wait(down, ag_recv.at[q, 2])
        send(lower, lower, ag_send.at[q], ag_recv.at[q, 7], along_z(-2))
        send(down, down, ag_send.at[q], ag_recv.at[q, 8], along_z(-1))
        to_sibling(q, -2)
        to_sibling(q, 2)
        wait(panels[q].at[at_z(-1)], ag_recv.at[q, 3])
        to_sibling(q, -1)
        wait(panels[q].at[at_z(1)], ag_recv.at[q, 4])
        to_sibling(q, 1)

    def spread(q, core):
        def one(at, carry):
            block = panels[q][core * 8 + at]
            both[core * 8 + at] = block
            both[16 + core * 8 + at] = turn(block.astype(F32)).astype(BF16)
            return carry

        lax.fori_loop(0, 8, one, 0, unroll=8)

    def gather_end(q):
        wait(panels[q].at[at_z(-3)], ag_recv.at[q, 6])
        to_sibling(q, -3)
        wait(panels[q].at[at_z(3)], ag_recv.at[q, 8])
        to_sibling(q, 3)
        wait(panels[q].at[at_z(4), pl.ds(0, HALF)], ag_recv.at[q, 5])
        wait(panels[q].at[at_z(4), pl.ds(HALF, HALF)], ag_recv.at[q, 7])
        to_sibling(q, 4)
        spread(q, k)
        wait(panels[q].at[pl.ds((1 - k) * 8, 8)], ag_recv.at[q, 0])
        spread(q, 1 - k)

    def products(q):
        def slot(t, total):
            product = jnp.dot(
                tiles[index_s[0, t]], both[index_s[1, t]], preferred_element_type=F32
            )
            total = jnp.where(index_s[2, t] > 0, product, total + product)
            running[t] = total
            return total

        lax.fori_loop(0, SLOTS, slot, jnp.zeros((T, T), F32), unroll=64)

    def scatter_start(q):
        def rows(to, start):
            return jnp.where(
                low[:HALF],
                running[index_s[3, to * 2], pl.ds(start, HALF)],
                running[index_s[3, to * 2 + 1], pl.ds(start, HALF)],
            ).astype(BF16)

        for step in (1, 3, 2, 0):
            for other in range(4):
                send_x[q, step, other] = rows(lax.rem(x + step, 4) * 4 + other, 0)
            if step:
                send(send_x.at[q, step], recv_x.at[q, step - 1],
                     rs_send.at[q, 0], rs_recv.at[q, 0], along_x(step))
            for other in range(4):
                send_y[q, step, other] = rows(other * 4 + lax.rem(y + step, 4), HALF)
            if step:
                send(send_y.at[q, step], recv_y.at[q, step - 1],
                     rs_send.at[q, 0], rs_recv.at[q, 1], along_y(step))

    def sum_of(own, got, q, at):
        return (
            own[q, 0, at].astype(F32) + got[q, 0, at].astype(F32)
            + got[q, 1, at].astype(F32) + got[q, 2, at].astype(F32)
        )

    def scatter_middle(q):
        wait(recv_x.at[q], rs_recv.at[q, 0])
        for step in (1, 3, 2):
            mid_x[q, step - 1] = sum_of(send_x, recv_x, q, lax.rem(y + step, 4)).astype(BF16)
            send(mid_x.at[q, step - 1], last_x.at[q, step - 1],
                 rs_send.at[q, 1], rs_recv.at[q, 2], along_y(step))
        wait(recv_y.at[q], rs_recv.at[q, 1])
        for step in (1, 3, 2):
            mid_y[q, step - 1] = sum_of(send_y, recv_y, q, lax.rem(x + step, 4)).astype(BF16)
            send(mid_y.at[q, step - 1], last_y.at[q, step - 1],
                 rs_send.at[q, 1], rs_recv.at[q, 3], along_x(step))
        part[q % 2, pl.ds(0, HALF), :] = sum_of(send_x, recv_x, q, y)
        part[q % 2, pl.ds(HALF, HALF), :] = sum_of(send_y, recv_y, q, x)

    def scatter_end(q):
        def total(last):
            return (
                last[q, 0].astype(F32) + last[q, 1].astype(F32) + last[q, 2].astype(F32)
            )

        wait(last_x.at[q], rs_recv.at[q, 2])
        part[q % 2, pl.ds(0, HALF), :] += total(last_x)
        wait(last_y.at[q], rs_recv.at[q, 3])
        part[q % 2, pl.ds(HALF, HALF), :] += total(last_y)
        held[q % 2] = -(s_b[...] * part[q % 2])

    def next_gather(q):
        scatter_end(q)
        put_block(q + 2, held[q % 2])
        gather_start(q + 2)

    def multiply(q):
        products(q)
        scatter_start(q)

    def reduce_start(g, xd, dd):
        pay[g, :, pl.ds(8, 8), :] = xd.reshape(16, 8, T)
        pay[g, :, 16, :] = dd

        def one(step, carry):
            to = lax.rem(r + step, 16)
            send(pay.at[g, to], got_a.at[g, step - 1],
                 ar_send.at[g, 0], ar_recv.at[g, 0], (to, c))
            return carry

        lax.fori_loop(1, 16, one, 0)

    def reduce_sibling(g):
        wait(got_a.at[g], ar_recv.at[g, 0])
        red_a[g] = pay[g, r] + jnp.sum(got_a[g], axis=0)
        send(red_a.at[g], got_s.at[g], ar_send.at[g, 1], ar_recv.at[g, 1], (r, sib))

    def reduce_z(g):
        wait(got_s.at[g], ar_recv.at[g, 1])
        red_b[g] = red_a[g] + got_s[g]

        def one(step, carry):
            send(red_b.at[g], got_b.at[g, step - 1],
                 ar_send.at[g, 2], ar_recv.at[g, 2], along_z(step))
            return carry

        lax.fori_loop(1, 8, one, 0)

    def reduce_share(g):
        wait(got_b.at[g], ar_recv.at[g, 2])
        got_c[g, r] = red_b[g] + jnp.sum(got_b[g], axis=0)

        def one(step, carry):
            mine_now = got_c.at[g, r]
            send(mine_now, mine_now, ar_send.at[g, 3], ar_recv.at[g, 3],
                 (lax.rem(r + step, 16), c))
            return carry

        lax.fori_loop(1, 16, one, 0)

    def reduce_end(g):
        wait(got_c.at[g, pl.ds(0, 15)], ar_recv.at[g, 3])
        xs = got_c[g, :, pl.ds(0, 8), :].reshape(T, T)
        xd = got_c[g, :, pl.ds(8, 8), :].reshape(T, T)
        dd = jnp.sum(got_c[g, :, 16, :], axis=0, keepdims=True)
        h = (xs + xd) * (1.0 / VERTS) - eye
        terms = h * mm(xs, h) - 2.0 * (h * xd)
        colsq = jnp.maximum(dd + jnp.sum(terms, axis=0, keepdims=True), 0.0)
        scale = lax.rsqrt(colsq * (1.0 / VERTS) + 1e-06)
        return h, jnp.sum(eye * scale, axis=1, keepdims=True)

    def squares(value):
        return jnp.sum((value * value).reshape(16, 16, T), axis=0)

    def order_slots():
        wide = (SLOTS, SLOTS)
        slots = lax.broadcasted_iota(jnp.int32, (1, SLOTS), 1)
        at_lane = lax.broadcasted_iota(jnp.int32, wide, 1)
        at_sub = lax.broadcasted_iota(jnp.int32, wide, 0)
        row = jnp.where(slots < live_ref[0, 0], rows_ref[...], 32)
        key = row * SLOTS + slots

        def column(value):
            spread = jnp.where(at_lane == at_sub, jnp.broadcast_to(value, wide), 0)
            return jnp.sum(spread, axis=1, keepdims=True)

        def count(mask, axis):
            return jnp.sum(mask.astype(jnp.int32), axis=axis, keepdims=True)

        row_c, key_c, col_c = column(row), column(key), column(cols_ref[...])
        rank = count(jnp.broadcast_to(key, wide) < key_c, 1)
        below = count(jnp.broadcast_to(row, wide) < row_c, 1)
        here = (rank == at_lane).astype(jnp.int32)
        turned = (row_c + col_c) % 2
        place = turned * 16 + (col_c // 2 % 2) * 8 + col_c // 4
        first_of = jnp.sum(here * below, axis=0, keepdims=True) == slots
        upto = count(row_c <= at_lane, 0)
        same = count(row_c == at_lane, 0)
        index_v[0:1, :] = jnp.sum(here * at_sub, axis=0, keepdims=True)
        index_v[1:2, :] = jnp.sum(here * place, axis=0, keepdims=True)
        index_v[2:3, :] = first_of.astype(jnp.int32)
        index_v[3:4, :] = jnp.where(same > 0, upto - 1, SLOTS)
        copy = pltpu.make_async_copy(index_v, index_s, index_sem)
        copy.start()
        copy.wait()

    loads[0].wait()
    for q, value in enumerate(pack(x_ref[pl.ds(0, T), :], x_ref[pl.ds(T, T), :])):
        put_block(q, value)
    pl.semaphore_wait(barrier, 23)

    gather_start(0)
    gather_start(1)
    for load in (2, 3, 7):
        loads[load].wait()
    order_slots()
    running[SLOTS] = jnp.zeros((T, T), F32)
    basis[:, pl.ds(0, T)] = x_ref[...]
    gather_middle(0)
    gather_middle(1)
    pay[0, :, pl.ds(0, 8), :] = gram_of(x_ref[...], x_ref[...]).reshape(16, 8, T)
    for load in (4, 5, 6):
        loads[load].wait()
    gather_end(0)
    multiply(0)
    gather_end(1)
    multiply(1)
    scatter_middle(0)
    scatter_middle(1)
    next_gather(0)
    next_gather(1)

    unpack(basis, T)
    d0 = basis[:, pl.ds(T, T)]
    reduce_start(0, gram_of(x_ref[...], d0), squares(d0))
    gather_middle(2)
    gather_middle(3)
    reduce_sibling(0)
    gather_end(2)
    multiply(2)
    reduce_z(0)
    gather_end(3)
    multiply(3)
    scatter_middle(2)
    reduce_share(0)
    scatter_middle(3)
    next_gather(2)
    next_gather(3)

    unpack(basis, 2 * T)
    h0, n0 = reduce_end(0)
    g1 = n0 * rot1_ref[pl.ds(T, T), :]
    h0g1 = mm(h0, g1)
    g_ref[pl.ds(0, T), :] = rot1_ref[pl.ds(0, T), :] - h0g1
    g_ref[pl.ds(T, T), :] = g1
    next_ref[:, pl.ds(0, T)] = mm(basis[:, pl.ds(0, 2 * T)], g_ref[...])
    next_ref[:, pl.ds(T, T)] = mm(basis[:, pl.ds(T, 2 * T)], g_ref[...])
    gather_middle(4)
    gather_middle(5)
    x1 = next_ref[:, pl.ds(0, T)]
    d1 = next_ref[:, pl.ds(T, T)]
    pay[1, :, pl.ds(0, 8), :] = gram_of(x1, x1).reshape(16, 8, T)
    reduce_start(1, gram_of(x1, d1), squares(d1))
    gather_end(4)
    reduce_sibling(1)
    multiply(4)
    reduce_z(1)
    gather_end(5)
    multiply(5)
    qp = rot2_ref[pl.ds(2 * T, T), :]
    q_ref[pl.ds(T, T), :] = mm(g_ref[pl.ds(T, T), :], qp)
    q_ref[pl.ds(0, T), :] = mm(g_ref[pl.ds(0, T), :] - rot1_ref[pl.ds(0, T), :], qp)
    block_ref[...] = mm(basis[:, pl.ds(0, 2 * T)], q_ref[...])
    image_ref[...] = mm(basis[:, pl.ds(T, 2 * T)], q_ref[...])
    scatter_middle(4)
    reduce_share(1)
    scatter_middle(5)
    h1, n1 = reduce_end(1)
    q1 = n1 * rot2_ref[pl.ds(T, T), :]
    q_ref[pl.ds(0, T), :] = rot2_ref[pl.ds(0, T), :] - mm(h1, q1)
    q_ref[pl.ds(T, T), :] = q1
    block_ref[...] += mm(next_ref[...], q_ref[...])
    image_ref[...] += mm(next_ref[:, pl.ds(T, T)], q_ref[pl.ds(0, T), :])
    q_ref[pl.ds(0, T), :] = mm(g_ref[pl.ds(0, T), :], q1)
    q_ref[pl.ds(T, T), :] = mm(g_ref[pl.ds(T, T), :], q1)
    image_ref[...] += mm(basis[:, pl.ds(2 * T, T)], q_ref[pl.ds(0, T), :])
    image_ref[...] += block_ref[...]
    scatter_end(4)
    scatter_end(5)
    unpack(last_ref, 0)
    image_ref[...] += mm(last_ref[...], q_ref[pl.ds(T, T), :])

    for q in range(CHAINS):
        wait(both.at[pl.ds(0, 15)], ag_send.at[q])
        wait(both.at[pl.ds(0, 12)], rs_send.at[q, 0])
        wait(both.at[pl.ds(0, 3)], rs_send.at[q, 1])
    for g in range(2):
        wait(got_a.at[g], ar_send.at[g, 0])
        wait(got_s.at[g], ar_send.at[g, 1])
        wait(got_b.at[g], ar_send.at[g, 2])
        wait(got_c.at[g, pl.ds(0, 15)], ar_send.at[g, 3])


def local(
    start_block, vertex_scale, adj_tiles, tile_row, tile_col, live_count,
    rotation_first, rotation_second,
):
    vmem = pl.BlockSpec(memory_space=pltpu.VMEM)
    hbm = pl.BlockSpec(memory_space=pl.ANY)
    tile = (T, T)
    out = jax.ShapeDtypeStruct((2 * T, T), F32)
    dma = pltpu.SemaphoreType.DMA
    return pl.pallas_call(
        kernel,
        out_shape=(out, out),
        in_specs=[hbm] * 8,
        out_specs=(vmem, vmem),
        scratch_shapes=[
            pltpu.VMEM((2 * T, T), F32),
            pltpu.VMEM((2, T), F32),
            pltpu.VMEM((1, SLOTS), jnp.int32),
            pltpu.VMEM((1, SLOTS), jnp.int32),
            pltpu.SMEM((1, 1), jnp.int32),
            pltpu.VMEM((2 * T, T), F32),
            pltpu.VMEM((3 * T, T), F32),
            pltpu.VMEM((SLOTS, *tile), BF16),
        ]
        + [pltpu.VMEM((16, *tile), BF16)] * CHAINS
        + [
            pltpu.VMEM((32, *tile), BF16),
            pltpu.VMEM((SLOTS + 1, *tile), F32),
            pltpu.VMEM((8, SLOTS), jnp.int32),
            pltpu.SMEM((8, SLOTS), jnp.int32),
        ]
        + [pltpu.VMEM(tile, F32), pltpu.VMEM((2, *tile), F32)]
        + [pltpu.VMEM((2 * T, 3 * T), F32), pltpu.VMEM((2 * T, 2 * T), F32)]
        + [pltpu.VMEM((2 * T, T), F32)] * 3
        + [pltpu.VMEM((2, *tile), F32)]
        + [pltpu.VMEM((CHAINS, 4, 4, HALF, T), BF16)] * 2
        + [pltpu.VMEM((CHAINS, 3, 4, HALF, T), BF16)] * 2
        + [pltpu.VMEM((CHAINS, 3, HALF, T), BF16)] * 4
        + [
            pltpu.VMEM((2, 16, ROWS, T), F32),
            pltpu.VMEM((2, ROWS, T), F32),
            pltpu.VMEM((2, 15, ROWS, T), F32),
            pltpu.VMEM((2, ROWS, T), F32),
            pltpu.VMEM((2, ROWS, T), F32),
            pltpu.VMEM((2, 7, ROWS, T), F32),
            pltpu.VMEM((2, 16, ROWS, T), F32),
            dma((8,)),
            dma,
            dma((CHAINS,)),
            dma((CHAINS, 9)),
            dma((CHAINS, 2)),
            dma((CHAINS, 4)),
            dma((2, 4)),
            dma((2, 4)),
        ],
        compiler_params=pltpu.CompilerParams(
            collective_id=0, has_side_effects=True, vmem_limit_bytes=60 << 20
        ),
        name="lobpcg",
    )(
        start_block,
        vertex_scale.reshape(2, T),
        adj_tiles[0, 0],
        tile_row[0],
        tile_col[0],
        live_count,
        rotation_first,
        rotation_second,
    )


def solution(mesh):
    placed = (
        P(("row", "col"), None),
        P(("row", "col")),
        P("row", "col", None, None, None),
        P("row", "col", None),
        P("row", "col", None),
        P("row", "col"),
        P(),
        P(),
    )
    return jax.shard_map(
        local,
        mesh=mesh,
        in_specs=placed,
        out_specs=(P(("row", "col"), None), P(("row", "col"), None)),
        check_vma=False,
    )
```

```python
import jax
import jax.numpy as jnp
from jax import lax
from jax.experimental import pallas as pl
from jax.experimental.pallas import tpu as pltpu
from jax.sharding import PartitionSpec as P

MESH = pl.DeviceIdType.MESH
HIGH = lax.Precision.HIGHEST
F32 = jnp.float32
BF16 = jnp.bfloat16
T = 128
SLOTS = 64
VERTS = 65536
HALF = 64
ROWS = 17
CHAINS = 6


def mm(left, right):
    return jnp.dot(left, right, precision=HIGH, preferred_element_type=F32)


def gram_of(left, right):
    return lax.dot_general(
        left, right, (((0,), (0,)), ((), ())), precision=HIGH, preferred_element_type=F32
    )


def kernel(
    x_hbm, scale_hbm, tiles_hbm, rows_hbm, cols_hbm, live_hbm, rot1_hbm, rot2_hbm,
    block_ref, image_ref,
    x_ref, scale_ref, rows_ref, cols_ref, live_ref, rot1_ref, rot2_ref,
    tiles, panel_0, panel_1, panel_2, panel_3, panel_4, panel_5, both, running, index_v, index_s, s_b, held, basis, next_ref, last_ref, g_ref, q_ref, part,
    send_x, send_y, recv_x, recv_y, mid_x, mid_y, last_x, last_y,
    pay, red_a, got_a, red_b, got_s, got_b, got_c,
    in_sem, index_sem, ag_send, ag_recv, rs_send, rs_recv, ar_send, ar_recv,
):
    panels = (panel_0, panel_1, panel_2, panel_3, panel_4, panel_5)
    r = lax.axis_index("row")
    c = lax.axis_index("col")
    x, y = r // 4, lax.rem(r, 4)
    z, k = c // 2, lax.rem(c, 2)
    sib = c + 1 - 2 * k

    def along_x(step):
        return (lax.rem(x + step, 4) * 4 + y, c)

    def along_y(step):
        return (x * 4 + lax.rem(y + step, 4), c)

    def along_z(step):
        return (r, lax.rem(z + step + 8, 8) * 2 + k)

    def send(src, dst, send_sem, recv_sem, device):
        pltpu.make_async_remote_copy(
            src_ref=src, dst_ref=dst, send_sem=send_sem, recv_sem=recv_sem,
            device_id=device, device_id_type=MESH,
        ).start()

    def wait(ref, sem):
        pltpu.make_async_copy(ref, ref, sem).wait()

    loads = [
        pltpu.make_async_copy(source, target, in_sem.at[at])
        for at, (source, target) in enumerate((
            (x_hbm, x_ref), (scale_hbm, scale_ref), (rows_hbm, rows_ref), (cols_hbm, cols_ref),
            (tiles_hbm, tiles), (rot1_hbm, rot1_ref), (rot2_hbm, rot2_ref), (live_hbm, live_ref),
        ))
    ]
    for load in loads:
        load.start()

    barrier = pltpu.get_barrier_semaphore()

    def greet_row(step, carry):
        pl.semaphore_signal(
            barrier, inc=1, device_id=(lax.rem(r + step, 16), c), device_id_type=MESH
        )
        return carry

    def greet_z(step, carry):
        pl.semaphore_signal(barrier, inc=1, device_id=along_z(step), device_id_type=MESH)
        return carry

    pl.semaphore_signal(barrier, inc=1, device_id=(r, sib), device_id_type=MESH)
    lax.fori_loop(1, 8, greet_z, 0)
    lax.fori_loop(1, 16, greet_row, 0)

    lane = lax.broadcasted_iota(jnp.int32, (T, T), 1)
    sub = lax.broadcasted_iota(jnp.int32, (T, T), 0)
    eye = (lane == sub).astype(F32)
    loads[1].wait()
    low = lane < HALF

    def turn(value):
        return pltpu.roll(value, HALF, 1)

    def scale_column(half):
        return jnp.sum(eye * scale_ref[pl.ds(half, 1), :], axis=1, keepdims=True)

    s_b[...] = jnp.where(low, scale_column(0), scale_column(1))

    def pack(top, bottom):
        return jnp.where(low, top, turn(bottom)), jnp.where(low, turn(top), bottom)

    def unpack(target, at):
        first, second = held[0], held[1]
        target[pl.ds(0, T), pl.ds(at, T)] = jnp.where(low, first, turn(second))
        target[pl.ds(T, T), pl.ds(at, T)] = jnp.where(low, turn(first), second)

    def at_z(step):
        return k * 8 + lax.rem(z + step + 8, 8)

    def put_block(q, value):
        panels[q][at_z(0)] = (s_b[...] * value).astype(BF16)

    def gather_start(q):
        own = panels[q].at[at_z(0)]
        send(own, own, ag_send.at[q], ag_recv.at[q, 1], along_z(2))
        send(own, own, ag_send.at[q], ag_recv.at[q, 2], along_z(-2))
        send(own, own, ag_send.at[q], ag_recv.at[q, 3], along_z(1))
        send(own, own, ag_send.at[q], ag_recv.at[q, 4], along_z(-1))
        send(own, own, ag_send.at[q], ag_recv.at[q, 0], (r, sib))

    def to_sibling(q, step):
        block = panels[q].at[at_z(step)]
        send(block, block, ag_send.at[q], ag_recv.at[q, 0], (r, sib))

    def gather_middle(q):
        up = panels[q].at[at_z(-2)]
        upper = panels[q].at[at_z(-2), pl.ds(0, HALF)]
        wait(up, ag_recv.at[q, 1])
        send(upper, upper, ag_send.at[q], ag_recv.at[q, 5], along_z(2))
        send(up, up, ag_send.at[q], ag_recv.at[q, 6], along_z(1))
        down = panels[q].at[at_z(2)]
        lower = panels[q].at[at_z(2), pl.ds(HALF, HALF)]
        wait(down, ag_recv.at[q, 2])
        send(lower, lower, ag_send.at[q], ag_recv.at[q, 7], along_z(-2))
        send(down, down, ag_send.at[q], ag_recv.at[q, 8], along_z(-1))
        to_sibling(q, -2)
        to_sibling(q, 2)
        wait(panels[q].at[at_z(-1)], ag_recv.at[q, 3])
        to_sibling(q, -1)
        wait(panels[q].at[at_z(1)], ag_recv.at[q, 4])
        to_sibling(q, 1)

    def spread(q, core):
        def one(at, carry):
            block = panels[q][core * 8 + at]
            both[core * 8 + at] = block
            both[16 + core * 8 + at] = turn(block.astype(F32)).astype(BF16)
            return carry

        lax.fori_loop(0, 8, one, 0, unroll=8)

    def gather_end(q):
        wait(panels[q].at[at_z(-3)], ag_recv.at[q, 6])
        to_sibling(q, -3)
        wait(panels[q].at[at_z(3)], ag_recv.at[q, 8])
        to_sibling(q, 3)
        wait(panels[q].at[at_z(4), pl.ds(0, HALF)], ag_recv.at[q, 5])
        wait(panels[q].at[at_z(4), pl.ds(HALF, HALF)], ag_recv.at[q, 7])
        to_sibling(q, 4)
        spread(q, k)
        wait(panels[q].at[pl.ds((1 - k) * 8, 8)], ag_recv.at[q, 0])
        spread(q, 1 - k)

    def products(q):
        def slot(t, total):
            product = jnp.dot(
                tiles[index_s[0, t]], both[index_s[1, t]], preferred_element_type=F32
            )
            total = jnp.where(index_s[2, t] > 0, product, total + product)
            running[t] = total
            return total

        lax.fori_loop(0, SLOTS, slot, jnp.zeros((T, T), F32), unroll=64)

    def scatter_start(q):
        def rows(to, start):
            return jnp.where(
                low[:HALF],
                running[index_s[3, to * 2], pl.ds(start, HALF)],
                running[index_s[3, to * 2 + 1], pl.ds(start, HALF)],
            ).astype(BF16)

        for step in (1, 3, 2, 0):
            for other in range(4):
                send_x[q, step, other] = rows(lax.rem(x + step, 4) * 4 + other, 0)
            if step:
                send(send_x.at[q, step], recv_x.at[q, step - 1],
                     rs_send.at[q, 0], rs_recv.at[q, 0], along_x(step))
            for other in range(4):
                send_y[q, step, other] = rows(other * 4 + lax.rem(y + step, 4), HALF)
            if step:
                send(send_y.at[q, step], recv_y.at[q, step - 1],
                     rs_send.at[q, 0], rs_recv.at[q, 1], along_y(step))

    def sum_of(own, got, q, at):
        return (
            own[q, 0, at].astype(F32) + got[q, 0, at].astype(F32)
            + got[q, 1, at].astype(F32) + got[q, 2, at].astype(F32)
        )

    def scatter_middle(q):
        wait(recv_x.at[q], rs_recv.at[q, 0])
        for step in (1, 3, 2):
            mid_x[q, step - 1] = sum_of(send_x, recv_x, q, lax.rem(y + step, 4)).astype(BF16)
            send(mid_x.at[q, step - 1], last_x.at[q, step - 1],
                 rs_send.at[q, 1], rs_recv.at[q, 2], along_y(step))
        wait(recv_y.at[q], rs_recv.at[q, 1])
        for step in (1, 3, 2):
            mid_y[q, step - 1] = sum_of(send_y, recv_y, q, lax.rem(x + step, 4)).astype(BF16)
            send(mid_y.at[q, step - 1], last_y.at[q, step - 1],
                 rs_send.at[q, 1], rs_recv.at[q, 3], along_x(step))
        part[q % 2, pl.ds(0, HALF), :] = sum_of(send_x, recv_x, q, y)
        part[q % 2, pl.ds(HALF, HALF), :] = sum_of(send_y, recv_y, q, x)

    def scatter_end(q):
        def total(last):
            return (
                last[q, 0].astype(F32) + last[q, 1].astype(F32) + last[q, 2].astype(F32)
            )

        wait(last_x.at[q], rs_recv.at[q, 2])
        part[q % 2, pl.ds(0, HALF), :] += total(last_x)
        wait(last_y.at[q], rs_recv.at[q, 3])
        part[q % 2, pl.ds(HALF, HALF), :] += total(last_y)
        held[q % 2] = -(s_b[...] * part[q % 2])

    def next_gather(q):
        scatter_end(q)
        put_block(q + 2, held[q % 2])
        gather_start(q + 2)

    def multiply(q):
        products(q)
        scatter_start(q)

    def reduce_start(g, xd, dd):
        pay[g, :, pl.ds(8, 8), :] = xd.reshape(16, 8, T)
        pay[g, :, 16, :] = dd

        def one(step, carry):
            to = lax.rem(r + step, 16)
            send(pay.at[g, to], got_a.at[g, step - 1],
                 ar_send.at[g, 0], ar_recv.at[g, 0], (to, c))
            return carry

        lax.fori_loop(1, 16, one, 0)

    def reduce_sibling(g):
        wait(got_a.at[g], ar_recv.at[g, 0])
        red_a[g] = pay[g, r] + jnp.sum(got_a[g], axis=0)
        send(red_a.at[g], got_s.at[g], ar_send.at[g, 1], ar_recv.at[g, 1], (r, sib))

    def reduce_z(g):
        wait(got_s.at[g], ar_recv.at[g, 1])
        red_b[g] = red_a[g] + got_s[g]

        def one(step, carry):
            send(red_b.at[g], got_b.at[g, step - 1],
                 ar_send.at[g, 2], ar_recv.at[g, 2], along_z(step))
            return carry

        lax.fori_loop(1, 8, one, 0)

    def reduce_share(g):
        wait(got_b.at[g], ar_recv.at[g, 2])
        got_c[g, r] = red_b[g] + jnp.sum(got_b[g], axis=0)

        def one(step, carry):
            mine_now = got_c.at[g, r]
            send(mine_now, mine_now, ar_send.at[g, 3], ar_recv.at[g, 3],
                 (lax.rem(r + step, 16), c))
            return carry

        lax.fori_loop(1, 16, one, 0)

    def reduce_end(g):
        wait(got_c.at[g, pl.ds(0, 15)], ar_recv.at[g, 3])
        xs = got_c[g, :, pl.ds(0, 8), :].reshape(T, T)
        xd = got_c[g, :, pl.ds(8, 8), :].reshape(T, T)
        dd = jnp.sum(got_c[g, :, 16, :], axis=0, keepdims=True)
        h = (xs + xd) * (1.0 / VERTS) - eye
        terms = h * mm(xs, h) - 2.0 * (h * xd)
        colsq = jnp.maximum(dd + jnp.sum(terms, axis=0, keepdims=True), 0.0)
        scale = lax.rsqrt(colsq * (1.0 / VERTS) + 1e-06)
        return h, jnp.sum(eye * scale, axis=1, keepdims=True)

    def squares(value):
        return jnp.sum((value * value).reshape(16, 16, T), axis=0)

    def order_slots():
        wide = (SLOTS, SLOTS)
        slots = lax.broadcasted_iota(jnp.int32, (1, SLOTS), 1)
        at_lane = lax.broadcasted_iota(jnp.int32, wide, 1)
        at_sub = lax.broadcasted_iota(jnp.int32, wide, 0)
        row = jnp.where(slots < live_ref[0, 0], rows_ref[...], 32)
        key = row * SLOTS + slots

        def column(value):
            spread = jnp.where(at_lane == at_sub, jnp.broadcast_to(value, wide), 0)
            return jnp.sum(spread, axis=1, keepdims=True)

        def count(mask, axis):
            return jnp.sum(mask.astype(jnp.int32), axis=axis, keepdims=True)

        row_c, key_c, col_c = column(row), column(key), column(cols_ref[...])
        rank = count(jnp.broadcast_to(key, wide) < key_c, 1)
        below = count(jnp.broadcast_to(row, wide) < row_c, 1)
        here = (rank == at_lane).astype(jnp.int32)
        turned = (row_c + col_c) % 2
        place = turned * 16 + (col_c // 2 % 2) * 8 + col_c // 4
        first_of = jnp.sum(here * below, axis=0, keepdims=True) == slots
        upto = count(row_c <= at_lane, 0)
        same = count(row_c == at_lane, 0)
        index_v[0:1, :] = jnp.sum(here * at_sub, axis=0, keepdims=True)
        index_v[1:2, :] = jnp.sum(here * place, axis=0, keepdims=True)
        index_v[2:3, :] = first_of.astype(jnp.int32)
        index_v[3:4, :] = jnp.where(same > 0, upto - 1, SLOTS)
        copy = pltpu.make_async_copy(index_v, index_s, index_sem)
        copy.start()
        copy.wait()

    loads[0].wait()
    for q, value in enumerate(pack(x_ref[pl.ds(0, T), :], x_ref[pl.ds(T, T), :])):
        put_block(q, value)
    pl.semaphore_wait(barrier, 23)

    gather_start(0)
    gather_start(1)
    for load in (2, 3, 7):
        loads[load].wait()
    order_slots()
    running[SLOTS] = jnp.zeros((T, T), F32)
    basis[:, pl.ds(0, T)] = x_ref[...]
    gather_middle(0)
    gather_middle(1)
    pay[0, :, pl.ds(0, 8), :] = gram_of(x_ref[...], x_ref[...]).reshape(16, 8, T)
    for load in (4, 5, 6):
        loads[load].wait()
    gather_end(0)
    multiply(0)
    gather_end(1)
    multiply(1)
    scatter_middle(0)
    scatter_middle(1)
    next_gather(0)
    next_gather(1)

    unpack(basis, T)
    d0 = basis[:, pl.ds(T, T)]
    reduce_start(0, gram_of(x_ref[...], d0), squares(d0))
    gather_middle(2)
    gather_middle(3)
    gather_end(2)
    multiply(2)
    reduce_sibling(0)
    gather_end(3)
    multiply(3)
    reduce_z(0)
    scatter_middle(2)
    scatter_middle(3)
    reduce_share(0)
    next_gather(2)
    next_gather(3)

    unpack(basis, 2 * T)
    h0, n0 = reduce_end(0)
    g1 = n0 * rot1_ref[pl.ds(T, T), :]
    h0g1 = mm(h0, g1)
    g_ref[pl.ds(0, T), :] = rot1_ref[pl.ds(0, T), :] - h0g1
    g_ref[pl.ds(T, T), :] = g1
    next_ref[:, pl.ds(0, T)] = mm(basis[:, pl.ds(0, 2 * T)], g_ref[...])
    next_ref[:, pl.ds(T, T)] = mm(basis[:, pl.ds(T, 2 * T)], g_ref[...])
    gather_middle(4)
    gather_middle(5)
    x1 = next_ref[:, pl.ds(0, T)]
    d1 = next_ref[:, pl.ds(T, T)]
    pay[1, :, pl.ds(0, 8), :] = gram_of(x1, x1).reshape(16, 8, T)
    reduce_start(1, gram_of(x1, d1), squares(d1))
    gather_end(4)
    reduce_sibling(1)
    multiply(4)
    reduce_z(1)
    gather_end(5)
    multiply(5)
    qp = rot2_ref[pl.ds(2 * T, T), :]
    q_ref[pl.ds(T, T), :] = mm(g_ref[pl.ds(T, T), :], qp)
    q_ref[pl.ds(0, T), :] = mm(g_ref[pl.ds(0, T), :] - rot1_ref[pl.ds(0, T), :], qp)
    block_ref[...] = mm(basis[:, pl.ds(0, 2 * T)], q_ref[...])
    image_ref[...] = mm(basis[:, pl.ds(T, 2 * T)], q_ref[...])
    scatter_middle(4)
    reduce_share(1)
    scatter_middle(5)
    h1, n1 = reduce_end(1)
    q1 = n1 * rot2_ref[pl.ds(T, T), :]
    q_ref[pl.ds(0, T), :] = rot2_ref[pl.ds(0, T), :] - mm(h1, q1)
    q_ref[pl.ds(T, T), :] = q1
    block_ref[...] += mm(next_ref[...], q_ref[...])
    image_ref[...] += mm(next_ref[:, pl.ds(T, T)], q_ref[pl.ds(0, T), :])
    q_ref[pl.ds(0, T), :] = mm(g_ref[pl.ds(0, T), :], q1)
    q_ref[pl.ds(T, T), :] = mm(g_ref[pl.ds(T, T), :], q1)
    image_ref[...] += mm(basis[:, pl.ds(2 * T, T)], q_ref[pl.ds(0, T), :])
    image_ref[...] += block_ref[...]
    scatter_end(4)
    scatter_end(5)
    unpack(last_ref, 0)
    image_ref[...] += mm(last_ref[...], q_ref[pl.ds(T, T), :])

    for q in range(CHAINS):
        wait(both.at[pl.ds(0, 15)], ag_send.at[q])
        wait(both.at[pl.ds(0, 12)], rs_send.at[q, 0])
        wait(both.at[pl.ds(0, 3)], rs_send.at[q, 1])
    for g in range(2):
        wait(got_a.at[g], ar_send.at[g, 0])
        wait(got_s.at[g], ar_send.at[g, 1])
        wait(got_b.at[g], ar_send.at[g, 2])
        wait(got_c.at[g, pl.ds(0, 15)], ar_send.at[g, 3])


def local(
    start_block, vertex_scale, adj_tiles, tile_row, tile_col, live_count,
    rotation_first, rotation_second,
):
    vmem = pl.BlockSpec(memory_space=pltpu.VMEM)
    hbm = pl.BlockSpec(memory_space=pl.ANY)
    tile = (T, T)
    out = jax.ShapeDtypeStruct((2 * T, T), F32)
    dma = pltpu.SemaphoreType.DMA
    return pl.pallas_call(
        kernel,
        out_shape=(out, out),
        in_specs=[hbm] * 8,
        out_specs=(vmem, vmem),
        scratch_shapes=[
            pltpu.VMEM((2 * T, T), F32),
            pltpu.VMEM((2, T), F32),
            pltpu.VMEM((1, SLOTS), jnp.int32),
            pltpu.VMEM((1, SLOTS), jnp.int32),
            pltpu.SMEM((1, 1), jnp.int32),
            pltpu.VMEM((2 * T, T), F32),
            pltpu.VMEM((3 * T, T), F32),
            pltpu.VMEM((SLOTS, *tile), BF16),
        ]
        + [pltpu.VMEM((16, *tile), BF16)] * CHAINS
        + [
            pltpu.VMEM((32, *tile), BF16),
            pltpu.VMEM((SLOTS + 1, *tile), F32),
            pltpu.VMEM((8, SLOTS), jnp.int32),
            pltpu.SMEM((8, SLOTS), jnp.int32),
        ]
        + [pltpu.VMEM(tile, F32), pltpu.VMEM((2, *tile), F32)]
        + [pltpu.VMEM((2 * T, 3 * T), F32), pltpu.VMEM((2 * T, 2 * T), F32)]
        + [pltpu.VMEM((2 * T, T), F32)] * 3
        + [pltpu.VMEM((2, *tile), F32)]
        + [pltpu.VMEM((CHAINS, 4, 4, HALF, T), BF16)] * 2
        + [pltpu.VMEM((CHAINS, 3, 4, HALF, T), BF16)] * 2
        + [pltpu.VMEM((CHAINS, 3, HALF, T), BF16)] * 4
        + [
            pltpu.VMEM((2, 16, ROWS, T), F32),
            pltpu.VMEM((2, ROWS, T), F32),
            pltpu.VMEM((2, 15, ROWS, T), F32),
            pltpu.VMEM((2, ROWS, T), F32),
            pltpu.VMEM((2, ROWS, T), F32),
            pltpu.VMEM((2, 7, ROWS, T), F32),
            pltpu.VMEM((2, 16, ROWS, T), F32),
            dma((8,)),
            dma,
            dma((CHAINS,)),
            dma((CHAINS, 9)),
            dma((CHAINS, 2)),
            dma((CHAINS, 4)),
            dma((2, 4)),
            dma((2, 4)),
        ],
        compiler_params=pltpu.CompilerParams(
            collective_id=0, has_side_effects=True, vmem_limit_bytes=60 << 20
        ),
        name="lobpcg",
    )(
        start_block,
        vertex_scale.reshape(2, T),
        adj_tiles[0, 0],
        tile_row[0],
        tile_col[0],
        live_count,
        rotation_first,
        rotation_second,
    )


def solution(mesh):
    placed = (
        P(("row", "col"), None),
        P(("row", "col")),
        P("row", "col", None, None, None),
        P("row", "col", None),
        P("row", "col", None),
        P("row", "col"),
        P(),
        P(),
    )
    return jax.shard_map(
        local,
        mesh=mesh,
        in_specs=placed,
        out_specs=(P(("row", "col"), None), P(("row", "col"), None)),
        check_vma=False,
    )
```
